128 devices in a mesh: leaf: 4 (over y), prow: 4 (over z), pcol: 8 (over x, core).
Axes of the slice: x: 4, y: 4, z: 4, core: 2. Of those that a mesh axis runs over, the one named last changes fastest.
Arguments:
- front_pivot: float32 [4, 1536, 1536], P('leaf', ('prow', 'pcol')), as said below
- front_lower: float32 [4, 6144, 1536], P('leaf', ('prow', 'pcol')), may hold values from -0.375 to 0.375
- front_rest: float32 [4, 6144, 6144], P('leaf', ('prow', 'pcol')), as said below
- parent_front: float32 [4, 8192, 4096], P('leaf', ('prow', 'pcol')), may hold values from -1.3 to 4.4, as said below
- relation: int32 [4, 6144], replicated, may hold values from 0 to 8191, as said below
Outputs:
- factor_pivot: float32 [4, 1536, 1536], P('leaf', ('prow', 'pcol'))
- factor_lower: float32 [4, 6144, 1536], P('leaf', ('prow', 'pcol'))
- parent_out: float32 [4, 8192, 4096], P('leaf', ('prow', 'pcol'))
The draws below stay inside these ranges and needn't reach their ends.
Inputs may be any that keep to these rules, and one draw needn't show every extreme that they name: Each front_pivot[g] is symmetric positive definite, with no eigenvalue under 0.3. Each front_rest[g] is symmetric, with diagonal entries between 6 and 9 and small off-diagonal entries. `parent_front`: the two column halves of one parent front together form a symmetric matrix. `relation`: for every front and every k, the entries k * 192 to (k + 1) * 192 - 1 rise strictly and lie in k * 256 to (k + 1) * 256 - 1, and take both ends of that range.
All inputs are finite; a program needn't handle non-finite values.
Results may differ from the reference program's by a relative error of at most 0.0029.
Values may be sent and summed in bfloat16 or wider, within the bound.
A program may use at most 128 MiB of HBM per device.

```python
import jax
import jax.numpy as jnp
from jax import lax

NS = 6144
NQ = 8192
NP = 1536
FRONTS = 4
RB = 192
WB = 256


def symmetric_front(key, pivot_order, low_diag, high_diag):
    first_key, second_key = jax.random.split(key, 2)
    shape = (FRONTS, pivot_order, pivot_order)
    noise_vals = jnp.clip(jax.random.normal(first_key, shape, jnp.float32), -6.0, 6.0)
    diagonal = jax.random.uniform(second_key, (FRONTS, pivot_order), jnp.float32, low_diag, high_diag)
    lower_part = jnp.tril(noise_vals, -1)
    symmetric = (lower_part + jnp.swapaxes(lower_part, 1, 2)) * (0.5 / pivot_order ** 0.5)
    return symmetric + diagonal[:, :, None] * jnp.eye(pivot_order, dtype=jnp.float32)[None]


def draw_front_pivot(key, part):
    inner_count = 2 * NP
    base_key = jax.random.fold_in(key, 11)
    shape = (FRONTS, NP, inner_count)
    entries = jnp.clip(jax.random.normal(base_key, shape, jnp.float32), -6.0, 6.0)
    gram = jnp.einsum('gik,gjk->gij', entries, entries, precision=lax.Precision.HIGHEST) * (3.0 / inner_count)
    symmetric = 0.5 * (gram + jnp.swapaxes(gram, 1, 2))
    return (symmetric + 0.3 * jnp.eye(NP, dtype=jnp.float32)[None]).astype(jnp.float32)


def draw_front_rest(key, part):
    return symmetric_front(jax.random.fold_in(key, 23), NS, 6.0, 9.0)


def draw_parent_front(key, part):
    half_cols = NQ // 2
    stride = max(NQ // 64, 2)
    parents = FRONTS // 2
    diag_key, near_key, far_key = jax.random.split(jax.random.fold_in(key, 53), 3)
    diag_vals = jax.random.uniform(diag_key, (parents, NQ), jnp.float32, 3.6, 4.4)
    near_vals = jax.random.uniform(near_key, (parents, NQ), jnp.float32, 0.7, 1.3)
    far_vals = jax.random.uniform(far_key, (parents, NQ), jnp.float32, 0.7, 1.3)
    rows = jnp.arange(NQ, dtype=jnp.int32)[:, None]
    halves = []
    for front_idx in range(FRONTS):
        parent = front_idx // 2
        side = front_idx % 2
        cols = side * half_cols + jnp.arange(half_cols, dtype=jnp.int32)[None, :]
        diag_row = diag_vals[parent][:, None]
        near_row = near_vals[parent][:, None]
        far_row = far_vals[parent][:, None]
        near_col = near_vals[parent][side * half_cols:(side + 1) * half_cols][None, :]
        far_col = far_vals[parent][side * half_cols:(side + 1) * half_cols][None, :]
        values = jnp.where(rows == cols, diag_row, 0.0)
        values = values - jnp.where(cols == rows + 1, near_row, 0.0)
        values = values - jnp.where(rows == cols + 1, near_col, 0.0)
        values = values - jnp.where(cols == rows + stride, far_row, 0.0)
        values = values - jnp.where(rows == cols + stride, far_col, 0.0)
        halves.append(values.astype(jnp.float32))
    return jnp.stack(halves)


def draw_relation(key, part):
    blocks = NS // RB
    block_keys = jax.random.split(jax.random.fold_in(key, 37), FRONTS * blocks)

    def one_block(sub_key):
        shuffled = jax.random.permutation(sub_key, WB - 2) + 1
        chosen_pos = jnp.sort(shuffled[:RB - 2]).astype(jnp.int32)
        return jnp.concatenate([jnp.zeros((1,), jnp.int32), chosen_pos, jnp.full((1,), WB - 1, jnp.int32)])
    chosen_all = jax.vmap(one_block)(block_keys)
    offsets = jnp.arange(FRONTS * blocks, dtype=jnp.int32) % blocks * WB
    return (chosen_all + offsets[:, None]).reshape(FRONTS, NS).astype(jnp.int32)


def level_of(stream_key, dims, cuts, least, high):
    gain, own = 1.0, jax.random.fold_in(stream_key, 6)
    for dim, parts in cuts:
        heights = jnp.exp(jax.random.uniform(jax.random.fold_in(own, dim), (parts,), jnp.float32, least / len(cuts), high / len(cuts)))
        gain = gain * jnp.repeat(heights, dims[dim] // parts).reshape([-1 if axis == dim else 1 for axis in range(len(dims))])
    return gain


def gaussian(stream_key, dims, spread, limit, shards=(), held_as=jnp.bfloat16):
    level = level_of(stream_key, dims, shards, -0.22, 0.18) if shards else 1.0
    array = jax.random.normal(stream_key, dims, jnp.float32) * spread * level
    return jnp.minimum(jnp.maximum(array, -limit), limit).astype(held_as)


def setup_inputs(seed: int = 0) -> dict:
    key_list = jax.random.split(jax.random.key(seed), 6)
    return {
        "front_pivot": draw_front_pivot(jax.random.fold_in(key_list[5], 71), 0),
        "front_lower": gaussian(key_list[1], (FRONTS, NS, NP), (NP // 6) ** -0.5, 0.375, ((0, 4), (1, 32)), jnp.float32),
        "front_rest": draw_front_rest(jax.random.fold_in(key_list[5], 71), 0),
        "parent_front": draw_parent_front(jax.random.fold_in(key_list[5], 71), 0),
        "relation": draw_relation(jax.random.fold_in(key_list[5], 71), 0),
    }


highest = lax.Precision.HIGHEST

def reference(front_pivot, front_lower, front_rest, parent_front, relation):
    pivots = []
    lowers = []
    schurs = []
    for front_idx in range(FRONTS):
        factor = jnp.linalg.cholesky(front_pivot[front_idx])
        lower_part = lax.linalg.triangular_solve(factor, front_lower[front_idx], left_side=False, lower=True, transpose_a=True)
        rounded = lax.optimization_barrier(lower_part.astype(jnp.bfloat16)).astype(jnp.float32)
        schur_block = front_rest[front_idx] - jnp.dot(rounded, rounded.T, precision=highest)
        pivots.append(factor)
        lowers.append(lower_part)
        schurs.append(schur_block)
    parent_halves = []
    for parent in range(FRONTS // 2):
        whole = jnp.concatenate([parent_front[2 * parent], parent_front[2 * parent + 1]], axis=1)
        for child_idx in (2 * parent, 2 * parent + 1):
            link_map = relation[child_idx].astype(jnp.int32)
            whole = whole.at[link_map[:, None], link_map[None, :]].add(schurs[child_idx])
        parent_halves.append(whole[:, :NQ // 2])
        parent_halves.append(whole[:, NQ // 2:])
    return (jnp.stack(pivots), jnp.stack(lowers), jnp.stack(parent_halves))
```

```python
import functools

import jax
import jax.numpy as jnp
from jax import lax
from jax.experimental import pallas as pl
from jax.experimental.pallas import tpu as pltpu
from jax.sharding import PartitionSpec as P

DB = 128
PB = 256
f32 = jnp.float32
bf16 = jnp.bfloat16


def two_terms(value):
    high = value.astype(bf16)
    low = (value - high.astype(f32)).astype(bf16)
    return high, low


def nt(a, b):
    return lax.dot_general(a, b, (((1,), (1,)), ((), ())), preferred_element_type=f32)


def nn(a, b):
    return lax.dot_general(a, b, (((1,), (0,)), ((), ())), preferred_element_type=f32)


def left3(value):
    high, low = two_terms(value)
    return jnp.concatenate([high, high, low], axis=1)


def right3(value, axis=1):
    high, low = two_terms(value)
    return jnp.concatenate([high, low, high], axis=axis)


def nt3(a, b):
    return nt(left3(a), right3(b))


def nn3(a, b):
    return nn(left3(a), right3(b, 0))


def factor_corner(work, segments=4):
    count = DB // 8
    sub = lax.broadcasted_iota(jnp.int32, (8, DB), 0)

    def step(first, block, carry):
        start = pl.multiple_of(block * 8, 8)
        rows_d = work[pl.ds(start, 8), :DB]
        rows_e = work[pl.ds(start, 8), DB:]
        lane = jnp.zeros((8, DB), jnp.int32) + start

        def column(rows, k):
            return jnp.take_along_axis(rows, lane + k, axis=1)

        a = {}
        for k in range(8):
            piece = column(rows_d, k)
            for s in range(k, 8):
                a[s, k] = jnp.broadcast_to(piece[s:s + 1], (8, DB))
        r = []
        up = []
        for i in range(8):
            inv = lax.rsqrt(a[i, i])
            r.append(inv)
            for k in range(i + 1, 8):
                a[k, i] = a[k, i] * inv
            for k in range(i + 1, 8):
                for j in range(i + 1, k + 1):
                    a[k, j] = a[k, j] - a[k, i] * a[j, i]
            pair = []
            for side, rows in enumerate((rows_d, rows_e)):
                value = jnp.broadcast_to(rows[i:i + 1], (8, DB))
                for k in range(i):
                    value = value - a[i, k] * up[k][side]
                pair.append(value * inv)
            up.append(pair)
        back = [None] * 8
        for i in reversed(range(8)):
            pair = []
            for side in range(2):
                value = up[i][side]
                for k in range(i + 1, 8):
                    value = value - a[k, i] * back[k][side]
                pair.append(value * r[i])
            back[i] = pair
        for side in range(2):
            value = up[0][side]
            for i in range(1, 8):
                value = jnp.where(sub == i, up[i][side], value)
            work[pl.ds(start, 8), side * DB:(side + 1) * DB] = value
        for v in range(first + 1, count):
            tile_d = work[v * 8:v * 8 + 8, :DB]
            tile_e = work[v * 8:v * 8 + 8, DB:]
            live = jnp.where(v > block, 1.0, 0.0).astype(f32)
            sum_d = sum_e = None
            for k in range(8):
                coef = column(tile_d, k)
                if k == 0:
                    sum_d = coef * back[k][0]
                    sum_e = coef * back[k][1]
                else:
                    sum_d = sum_d + coef * back[k][0]
                    sum_e = sum_e + coef * back[k][1]
            work[v * 8:v * 8 + 8, :DB] = tile_d - live * sum_d
            work[v * 8:v * 8 + 8, DB:] = tile_e - live * sum_e
        return carry

    size = count // segments
    for seg in range(segments):
        lax.fori_loop(seg * size, (seg + 1) * size, lambda b, c, f=seg * size: step(f, b, c), 0)


def factor_kernel(order, rows, where_ref, a_ref, b_ref, l_ref, x_ref, g_ref, m, work, inv, p_hi, p_lo):
    total = order + rows
    eye = (lax.broadcasted_iota(jnp.int32, (DB, DB), 0) == lax.broadcasted_iota(jnp.int32, (DB, DB), 1)).astype(f32)
    low_mask = lax.broadcasted_iota(jnp.int32, (DB, DB), 0) >= lax.broadcasted_iota(jnp.int32, (DB, DB), 1)
    m[:order, :] = a_ref[...]
    m[order:, :] = b_ref[...]
    zero = jnp.zeros((DB, DB), f32)
    for p in range(order // PB):
        c0 = p * PB
        c1 = c0 + DB
        c2 = c0 + PB
        work[:, :DB] = m[c0:c1, c0:c1]
        work[:, DB:] = eye
        factor_corner(work)
        l11 = jnp.where(low_mask, work[:, :DB].T, 0.0)
        i11 = work[:, DB:]
        l21 = nt3(m[c1:c2, c0:c1], i11)
        work[:, :DB] = m[c1:c2, c1:c2] - nt3(l21, l21)
        work[:, DB:] = eye
        factor_corner(work)
        l22 = jnp.where(low_mask, work[:, :DB].T, 0.0)
        i22 = work[:, DB:]
        i21 = -nn3(i22, nn3(l21, i11))
        m[c0:c1, c0:c1] = l11
        m[c0:c1, c1:c2] = zero
        m[c1:c2, c0:c1] = l21
        m[c1:c2, c1:c2] = l22
        inv[c0:c1, :DB] = i11
        inv[c0:c1, DB:] = zero
        inv[c1:c2, :DB] = i21
        inv[c1:c2, DB:] = i22
        panel = nt3(m[c2:, c0:c2], inv[c0:c2, :])
        m[c2:, c0:c2] = panel
        hi, lo = two_terms(panel)
        p_hi[c2:, :] = hi
        p_lo[c2:, :] = lo
        for j in range(c2, order, PB):
            right = jnp.concatenate([p_hi[j:j + PB], p_lo[j:j + PB], p_hi[j:j + PB]], axis=1)
            left = jnp.concatenate([p_hi[j:], p_hi[j:], p_lo[j:]], axis=1)
            m[j:, j:j + PB] = m[j:, j:j + PB] - nt(left, right)
    x_ref[...] = m[order:, :]
    held = l_ref.shape[0]
    top = pl.multiple_of(where_ref[0] * held, 8)
    own = m[pl.ds(top, held), :]
    row_id = lax.broadcasted_iota(jnp.int32, own.shape, 0) + top
    col_id = lax.broadcasted_iota(jnp.int32, own.shape, 1)
    l_ref[...] = jnp.where(col_id <= row_id, own, 0.0)
    for p in reversed(range(order // PB)):
        c0 = p * PB
        c2 = c0 + PB
        rhs = m[order:, c0:c2]
        if c2 < order:
            rhs = rhs - nn3(m[order:, c2:], m[c2:order, c0:c2])
        g = nn3(rhs, inv[c0:c2, :])
        m[order:, c0:c2] = g
        g_ref[:, c0:c2] = g.astype(bf16)


def factor(where, a, b, held):
    order = a.shape[0]
    rows = b.shape[0]
    vm = pl.BlockSpec(memory_space=pltpu.VMEM)
    return pl.pallas_call(
        functools.partial(factor_kernel, order, rows),
        out_shape=(
            jax.ShapeDtypeStruct((held, order), f32),
            jax.ShapeDtypeStruct((rows, order), f32),
            jax.ShapeDtypeStruct((rows, order), bf16),
        ),
        in_specs=[pl.BlockSpec(memory_space=pltpu.SMEM), vm, vm],
        out_specs=(vm, vm, vm),
        scratch_shapes=[
            pltpu.VMEM((order + rows, order), f32),
            pltpu.VMEM((DB, 2 * DB), f32),
            pltpu.VMEM((order, PB), f32),
            pltpu.VMEM((order + rows, PB), bf16),
            pltpu.VMEM((order + rows, PB), bf16),
        ],
        compiler_params=pltpu.CompilerParams(vmem_limit_bytes=60 * 2**20),
        cost_estimate=pl.CostEstimate(flops=100 * 10**9, bytes_accessed=2 * 10**7, transcendentals=0),
        name="factor",
    )(where, a, b)


def assemble_kernel(pick, g_ref, b_ref, c_ref, rows_ref, cols_ref, base_ref, out_ref):
    height = base_ref.shape[0]
    width = base_ref.shape[1]
    schur = c_ref[...].astype(f32) - nt(g_ref[...], b_ref[...])
    high, low = two_terms(schur)
    spot = lax.broadcasted_iota(jnp.int32, (width, high.shape[1]), 0)
    col_table = (spot == cols_ref[0]).astype(bf16)
    spot = lax.broadcasted_iota(jnp.int32, (height, high.shape[0]), 0)
    row_table = (spot == rows_ref[...]).astype(bf16)
    high = nt(high, col_table).astype(bf16)
    low = nt(low, col_table).astype(bf16)
    out_ref[...] = base_ref[...] + (nn(row_table, high) + nn(row_table, low))


def assemble(pick, g, b_all, c, row_link, col_link, base):
    steps, _, wide = col_link.shape
    rows, order = g.shape
    height, full = base.shape
    window = full // steps
    return pl.pallas_call(
        assemble_kernel,
        out_shape=jax.ShapeDtypeStruct(base.shape, f32),
        grid_spec=pltpu.PrefetchScalarGridSpec(
            num_scalar_prefetch=1,
            grid=(steps,),
            in_specs=[
                pl.BlockSpec((rows, order), lambda t, pick: (0, 0)),
                pl.BlockSpec((wide, order), lambda t, pick: (pick[0] + t, 0)),
                pl.BlockSpec((rows, wide), lambda t, pick: (0, pick[1] + t)),
                pl.BlockSpec((1, rows), lambda t, pick: (0, 0)),
                pl.BlockSpec((1, 1, wide), lambda t, pick: (t, 0, 0)),
                pl.BlockSpec((height, window), lambda t, pick: (0, t)),
            ],
            out_specs=pl.BlockSpec((height, window), lambda t, pick: (0, t)),
        ),
        input_output_aliases={6: 0},
        cost_estimate=pl.CostEstimate(flops=5 * 10**9, bytes_accessed=2 * 10**7, transcendentals=0),
        name="assemble",
    )(pick, g, b_all, c, row_link, col_link, base)


AXES = ("leaf", "prow", "pcol")


def local(front_pivot, front_lower, front_rest, parent_front, relation):
    position = lax.axis_index(("prow", "pcol"))
    leaf = lax.axis_index("leaf")
    spots = lax.axis_size("prow") * lax.axis_size("pcol")
    leaves = lax.axis_size("leaf")
    half_spots = spots // 2
    side = leaf % 2
    partner = leaf + 1 - 2 * side
    pivot_rows = front_pivot[0]
    lower_rows = front_lower[0]
    rest_rows = front_rest[0]
    base = parent_front[0]
    rows_here, child_order = rest_rows.shape
    half = child_order // 2
    height, parent_half = base.shape
    steps = 8
    wide = half // steps
    window = parent_half // steps

    matrix = lax.all_gather(pivot_rows, ("prow", "pcol"), axis=0, tiled=True)

    low_bits = lower_rows.astype(bf16)
    swap = []
    mirror = []
    for one in range(leaves):
        for spot in range(spots):
            mirror.append((one * spots + spot, (one ^ 1) * spots + spot))
            if spot // half_spots != one % 2:
                swap.append((one * spots + spot, (one ^ 1) * spots + (spot ^ half_spots)))
    swapped = lax.ppermute(low_bits, AXES, swap)
    block = jnp.where(position // half_spots == side, low_bits, swapped)
    b_all = lax.all_gather(block, ("prow", "pcol"), axis=0, tiled=True)
    other = lax.dynamic_slice_in_dim(rest_rows, (1 - side) * half, half, 1).astype(bf16)
    rest_sib = lax.ppermute(other, AXES, mirror)

    where = jnp.full((1,), position, jnp.int32)
    pivot_out, lower_out, g = factor(where, matrix, lower_rows, pivot_rows.shape[0])
    g_sib = lax.ppermute(g, AXES, mirror)

    def links(child):
        link = lax.dynamic_index_in_dim(relation, child, 0, keepdims=False)
        row_link = lax.dynamic_slice_in_dim(link, position * rows_here, rows_here, 0) - position * height
        col_link = lax.dynamic_slice_in_dim(link, side * half, half, 0) - side * parent_half
        col_link = col_link.reshape(steps, 1, wide) - jnp.arange(steps, dtype=jnp.int32)[:, None, None] * window
        return row_link[None], col_link

    row_own, col_own = links(leaf)
    row_sib, col_sib = links(partner)
    pick_own = jnp.stack([side * steps, side * steps]).astype(jnp.int32)
    pick_sib = jnp.stack([(1 - side) * steps, 0 * side]).astype(jnp.int32)
    merged = assemble(pick_own, g, b_all, rest_rows, row_own, col_own, base)
    merged = assemble(pick_sib, g_sib, b_all, rest_sib, row_sib, col_sib, merged)
    return (pivot_out[None], lower_out[None], merged[None])


def solution(mesh):
    spec = P("leaf", ("prow", "pcol"), None)
    return jax.shard_map(
        local,
        mesh=mesh,
        in_specs=(spec, spec, spec, spec, P()),
        out_specs=(spec, spec, spec),
        check_vma=False,
    )
```

```python
import functools

import jax
import jax.numpy as jnp
from jax import lax
from jax.experimental import pallas as pl
from jax.experimental.pallas import tpu as pltpu
from jax.sharding import PartitionSpec as P

DB = 128
PB = 256
f32 = jnp.float32
bf16 = jnp.bfloat16


def two_terms(value):
    high = value.astype(bf16)
    low = (value - high.astype(f32)).astype(bf16)
    return high, low


def nt(a, b):
    return lax.dot_general(a, b, (((1,), (1,)), ((), ())), preferred_element_type=f32)


def nn(a, b):
    return lax.dot_general(a, b, (((1,), (0,)), ((), ())), preferred_element_type=f32)


def left3(value):
    high, low = two_terms(value)
    return jnp.concatenate([high, high, low], axis=1)


def right3(value, axis=1):
    high, low = two_terms(value)
    return jnp.concatenate([high, low, high], axis=axis)


def nt3(a, b):
    return nt(left3(a), right3(b))


def nn3(a, b):
    return nn(left3(a), right3(b, 0))


def factor_corner(work, keep, segments=2):
    count = DB // 8
    sub = lax.broadcasted_iota(jnp.int32, (8, DB), 0)

    def wide(row):
        return jnp.broadcast_to(row, (8, DB))

    def step(first, block, carry):
        start = pl.multiple_of(block * 8, 8)
        after = pl.multiple_of(start + 8, 8)
        before = pl.multiple_of(jnp.maximum(start - 8, 0), 8)
        started = jnp.where(block > 0, 1.0, 0.0).astype(f32)
        halves = (slice(0, DB), slice(DB, 2 * DB))
        rows = [work[pl.ds(start, 8), h] for h in halves]
        tile = [work[pl.ds(after, 8), h] for h in halves]
        past = [keep[pl.ds(before, 8), h] for h in halves]
        lane = jnp.zeros((8, DB), jnp.int32) + start
        lane_before = jnp.zeros((8, DB), jnp.int32) + before

        low = (first + 1) * 8
        if low < DB:
            left = work[low:DB, :DB]
            place = lax.broadcasted_iota(jnp.int32, left.shape, 1)
            depth = lax.broadcasted_iota(jnp.int32, left.shape, 0) + low
            chosen = (place >= start - 8) & (place < start) & (depth >= start + 16)
            left = jnp.where(chosen, left, 0.0)
            change = nn3(left, keep[...])

        for k in range(8):
            coef = jnp.take_along_axis(tile[0], lane_before + k, axis=1) * started
            if k == 0:
                drop = [coef * wide(past[s][k:k + 1]) for s in range(2)]
            else:
                drop = [drop[s] + coef * wide(past[s][k:k + 1]) for s in range(2)]
        tile = [tile[s] - drop[s] for s in range(2)]

        a = {}
        side_col = []
        for k in range(8):
            piece = jnp.take_along_axis(rows[0], lane + k, axis=1)
            for s in range(k, 8):
                a[s, k] = wide(piece[s:s + 1])
            side_col.append(jnp.take_along_axis(tile[0], lane + k, axis=1))
        r = []
        up = []
        for i in range(8):
            inv = lax.rsqrt(a[i, i])
            r.append(inv)
            for k in range(i + 1, 8):
                a[k, i] = a[k, i] * inv
            for k in range(i + 1, 8):
                for j in range(i + 1, k + 1):
                    a[k, j] = a[k, j] - a[k, i] * a[j, i]
            side_col[i] = side_col[i] * inv
            for k in range(i + 1, 8):
                side_col[k] = side_col[k] - a[k, i] * side_col[i]
            if i == 0:
                run = [[wide(rows[s][k:k + 1]) for k in range(8)] for s in range(2)]
            pair = []
            for s in range(2):
                value = run[s][i] * inv
                pair.append(value)
                for k in range(i + 1, 8):
                    run[s][k] = run[s][k] - a[k, i] * value
                tile[s] = tile[s] - side_col[i] * value
            up.append(pair)
        if low < DB:
            work[low:DB, :] = work[low:DB, :] - change
        for s in range(2):
            work[pl.ds(after, 8), halves[s]] = tile[s]
            value = up[0][s]
            for i in range(1, 8):
                value = jnp.where(sub == i, up[i][s], value)
            work[pl.ds(start, 8), halves[s]] = value
        back = [None] * 8
        for i in reversed(range(8)):
            pair = []
            for s in range(2):
                value = up[i][s]
                for k in range(i + 1, 8):
                    value = value - a[k, i] * back[k][s]
                pair.append(value * r[i])
            back[i] = pair
        for s in range(2):
            value = back[0][s]
            for i in range(1, 8):
                value = jnp.where(sub == i, back[i][s], value)
            keep[pl.ds(start, 8), halves[s]] = value
        return carry

    size = count // segments
    for seg in range(segments):
        lax.fori_loop(seg * size, (seg + 1) * size, lambda b, c, f=seg * size: step(f, b, c), 0)


def factor_kernel(order, rows, where_ref, a_ref, b_ref, l_ref, x_ref, g_ref, m, work, keep, inv, p_hi, p_lo, fetch_sem):
    total = order + rows
    eye = (lax.broadcasted_iota(jnp.int32, (DB, DB), 0) == lax.broadcasted_iota(jnp.int32, (DB, DB), 1)).astype(f32)
    low_mask = lax.broadcasted_iota(jnp.int32, (DB, DB), 0) >= lax.broadcasted_iota(jnp.int32, (DB, DB), 1)
    fetch = pltpu.make_async_copy(a_ref, m.at[:order, :], fetch_sem)
    fetch.start()
    m[order:, :] = b_ref[...]
    zero = jnp.zeros((DB, DB), f32)
    keep[...] = jnp.zeros_like(keep)
    work[DB:, :] = jnp.zeros((8, 2 * DB), f32)
    fetch.wait()
    for p in range(order // PB):
        c0 = p * PB
        c1 = c0 + DB
        c2 = c0 + PB
        work[:DB, :DB] = m[c0:c1, c0:c1]
        work[:DB, DB:] = eye
        factor_corner(work, keep)
        l11 = jnp.where(low_mask, work[:DB, :DB].T, 0.0)
        i11 = work[:DB, DB:]
        l21 = nt3(m[c1:c2, c0:c1], i11)
        work[:DB, :DB] = m[c1:c2, c1:c2] - nt3(l21, l21)
        work[:DB, DB:] = eye
        factor_corner(work, keep)
        l22 = jnp.where(low_mask, work[:DB, :DB].T, 0.0)
        i22 = work[:DB, DB:]
        i21 = -nn3(i22, nn3(l21, i11))
        m[c0:c1, c0:c1] = l11
        m[c0:c1, c1:c2] = zero
        m[c1:c2, c0:c1] = l21
        m[c1:c2, c1:c2] = l22
        inv[c0:c1, :DB] = i11
        inv[c0:c1, DB:] = zero
        inv[c1:c2, :DB] = i21
        inv[c1:c2, DB:] = i22
        panel = nt3(m[c2:, c0:c2], inv[c0:c2, :])
        m[c2:, c0:c2] = panel
        hi, lo = two_terms(panel)
        p_hi[c2:, :] = hi
        p_lo[c2:, :] = lo
        for j in range(c2, order, PB):
            right = jnp.concatenate([p_hi[j:j + PB], p_lo[j:j + PB], p_hi[j:j + PB]], axis=1)
            left = jnp.concatenate([p_hi[j:], p_hi[j:], p_lo[j:]], axis=1)
            m[j:, j:j + PB] = m[j:, j:j + PB] - nt(left, right)
    x_ref[...] = m[order:, :]
    held = l_ref.shape[0]
    top = pl.multiple_of(where_ref[0] * held, 8)
    own = m[pl.ds(top, held), :]
    row_id = lax.broadcasted_iota(jnp.int32, own.shape, 0) + top
    col_id = lax.broadcasted_iota(jnp.int32, own.shape, 1)
    l_ref[...] = jnp.where(col_id <= row_id, own, 0.0)
    for p in reversed(range(order // PB)):
        c0 = p * PB
        c2 = c0 + PB
        rhs = m[order:, c0:c2]
        if c2 < order:
            rhs = rhs - nn3(m[order:, c2:], m[c2:order, c0:c2])
        g = nn3(rhs, inv[c0:c2, :])
        m[order:, c0:c2] = g
        g_ref[:, c0:c2] = g.astype(bf16)


MESH = pl.DeviceIdType.MESH


def gather_kernel(own_ref, out_ref, send, local_sem, recv_f, recv_s, recv_c):
    rows = own_ref.shape[0]
    part = rows // 2
    leaf = lax.axis_index("leaf")
    z = lax.axis_index("prow")
    pcol = lax.axis_index("pcol")
    size = 4
    x = pcol // 2
    core = pcol % 2
    flip = core == 1
    f = jnp.where(flip, z, x)
    s = jnp.where(flip, x, z)

    def device(fi, si, ci):
        zi = jnp.where(flip, fi, si)
        xi = jnp.where(flip, si, fi)
        return (leaf, zi, xi * 2 + ci)

    def first(fi, si):
        zi = jnp.where(flip, fi, si)
        xi = jnp.where(flip, si, fi)
        return (zi * 2 * size + xi * 2 + core) * rows

    def window(fi, si, piece):
        top = first(fi, si)
        if piece is None:
            return out_ref.at[pl.ds(pl.multiple_of(top, 8), rows), :]
        return out_ref.at[pl.ds(pl.multiple_of(top + piece * part, 8), part), :]

    def near(v, d):
        return (v + d + size) % size

    f_dev = [device(near(f, 1), s, core), device(near(f, -1), s, core)]
    s_dev = [device(f, near(s, 1), core), device(f, near(s, -1), core)]
    twin = device(f, s, 1 - core)

    barrier = pltpu.get_barrier_semaphore()
    for dev in f_dev + s_dev + [twin]:
        pl.semaphore_signal(barrier, inc=1, device_id=dev, device_id_type=MESH)
    pl.semaphore_wait(barrier, 5)

    started = []

    def push(src, dst, recv_sem, dev):
        copy = pltpu.make_async_remote_copy(
            src_ref=src, dst_ref=dst, send_sem=send.at[len(started)], recv_sem=recv_sem,
            device_id=dev, device_id_type=MESH,
        )
        copy.start()
        started.append(copy)

    def arrived(dst, recv_sem):
        pltpu.make_async_remote_copy(
            src_ref=dst, dst_ref=dst, send_sem=send.at[0], recv_sem=recv_sem,
            device_id=twin, device_id_type=MESH,
        ).wait_recv()

    offsets = [0, -1, 1, 2]

    def pass_on(k, src, fi):
        dst = window(fi, s, None)
        for d in range(2):
            push(src, dst, recv_s.at[k, d], s_dev[d])
        push(src, dst, recv_c.at[0, k], twin)

    own_dst = window(f, s, None)
    for d in range(2):
        push(own_ref, own_dst, recv_f.at[d], f_dev[d])
    pass_on(0, own_ref, f)
    keep = pltpu.make_async_copy(own_ref, own_dst, local_sem)
    keep.start()

    for d, off in ((0, -1), (1, 1)):
        fi = near(f, off)
        arrived(window(fi, s, None), recv_f.at[d])
        push(window(fi, s, d), window(fi, s, d), recv_f.at[2 + d], f_dev[d])
        pass_on(1 + d, window(fi, s, None), fi)

    def second(k):
        fi = near(f, offsets[k])
        for d, off in ((0, -1), (1, 1)):
            si = near(s, off)
            arrived(window(fi, si, None), recv_s.at[k, d])
            push(window(fi, si, d), window(fi, si, d), recv_s.at[k, 2 + d], s_dev[d])
            push(window(fi, si, None), window(fi, si, None), recv_c.at[1 + d, k], twin)

    def third(k):
        fi = near(f, offsets[k])
        si = near(s, 2)
        for d in range(2):
            arrived(window(fi, si, d), recv_s.at[k, 2 + d])
        push(window(fi, si, None), window(fi, si, None), recv_c.at[3, k], twin)

    second(0)
    fi = near(f, 2)
    for d in range(2):
        arrived(window(fi, s, d), recv_f.at[2 + d])
    pass_on(3, window(fi, s, None), fi)
    second(1)
    third(0)
    second(2)
    third(1)
    second(3)
    third(2)
    third(3)

    def twin_window(a, b):
        tf, ts = s, f
        fi = near(tf, offsets[b])
        si = near(ts, (0, -1, 1, 2)[a])
        zi = jnp.where(flip, si, fi)
        xi = jnp.where(flip, fi, si)
        top = (zi * 2 * size + xi * 2 + (1 - core)) * rows
        return out_ref.at[pl.ds(pl.multiple_of(top, 8), rows), :]

    for a in range(4):
        for b in range(4):
            arrived(twin_window(a, b), recv_c.at[a, b])
    for copy in started:
        copy.wait_send()
    keep.wait()


def gather_rows(own, count):
    any_spec = pl.BlockSpec(memory_space=pl.ANY)
    return pl.pallas_call(
        gather_kernel,
        out_shape=jax.ShapeDtypeStruct((own.shape[0] * count, own.shape[1]), own.dtype),
        in_specs=[any_spec],
        out_specs=any_spec,
        scratch_shapes=[
            pltpu.SemaphoreType.DMA((40,)),
            pltpu.SemaphoreType.DMA,
            pltpu.SemaphoreType.DMA((4,)),
            pltpu.SemaphoreType.DMA((4, 4)),
            pltpu.SemaphoreType.DMA((4, 4)),
        ],
        compiler_params=pltpu.CompilerParams(collective_id=0, has_side_effects=True),
        name="gather_rows",
    )(own)


def factor(where, a, b, held):
    order = a.shape[0]
    rows = b.shape[0]
    vm = pl.BlockSpec(memory_space=pltpu.VMEM)
    return pl.pallas_call(
        functools.partial(factor_kernel, order, rows),
        out_shape=(
            jax.ShapeDtypeStruct((held, order), f32),
            jax.ShapeDtypeStruct((rows, order), f32),
            jax.ShapeDtypeStruct((rows, order), bf16),
        ),
        in_specs=[pl.BlockSpec(memory_space=pltpu.SMEM), pl.BlockSpec(memory_space=pl.ANY), vm],
        out_specs=(vm, vm, vm),
        scratch_shapes=[
            pltpu.VMEM((order + rows, order), f32),
            pltpu.VMEM((DB + 8, 2 * DB), f32),
            pltpu.VMEM((DB, 2 * DB), f32),
            pltpu.VMEM((order, PB), f32),
            pltpu.VMEM((order + rows, PB), bf16),
            pltpu.VMEM((order + rows, PB), bf16),
            pltpu.SemaphoreType.DMA,
        ],
        compiler_params=pltpu.CompilerParams(vmem_limit_bytes=60 * 2**20),
        cost_estimate=pl.CostEstimate(flops=70 * 10**9, bytes_accessed=2 * 10**7, transcendentals=0),
        name="factor",
    )(where, a, b)


def assemble_kernel(pick, g_ref, b_ref, c_ref, rows_ref, cols_ref, base_ref, out_ref):
    height = base_ref.shape[0]
    width = base_ref.shape[1]
    schur = c_ref[...].astype(f32) - nt(g_ref[...], b_ref[...])
    high, low = two_terms(schur)
    spot = lax.broadcasted_iota(jnp.int32, (width, high.shape[1]), 0)
    col_table = (spot == cols_ref[0]).astype(bf16)
    spot = lax.broadcasted_iota(jnp.int32, (height, high.shape[0]), 0)
    row_table = (spot == rows_ref[...]).astype(bf16)
    high = nt(high, col_table).astype(bf16)
    low = nt(low, col_table).astype(bf16)
    out_ref[...] = base_ref[...] + (nn(row_table, high) + nn(row_table, low))


def assemble(pick, g, b_all, c, row_link, col_link, base):
    steps, _, wide = col_link.shape
    rows, order = g.shape
    height, full = base.shape
    window = full // steps
    return pl.pallas_call(
        assemble_kernel,
        out_shape=jax.ShapeDtypeStruct(base.shape, f32),
        grid_spec=pltpu.PrefetchScalarGridSpec(
            num_scalar_prefetch=1,
            grid=(steps,),
            in_specs=[
                pl.BlockSpec((rows, order), lambda t, pick: (0, 0)),
                pl.BlockSpec((wide, order), lambda t, pick: (pick[0] + t, 0)),
                pl.BlockSpec((rows, wide), lambda t, pick: (0, pick[1] + t)),
                pl.BlockSpec((1, rows), lambda t, pick: (0, 0)),
                pl.BlockSpec((1, 1, wide), lambda t, pick: (t, 0, 0)),
                pl.BlockSpec((height, window), lambda t, pick: (0, t)),
            ],
            out_specs=pl.BlockSpec((height, window), lambda t, pick: (0, t)),
        ),
        input_output_aliases={6: 0},
        cost_estimate=pl.CostEstimate(flops=5 * 10**9, bytes_accessed=2 * 10**7, transcendentals=0),
        name="assemble",
    )(pick, g, b_all, c, row_link, col_link, base)


AXES = ("leaf", "prow", "pcol")


def local(front_pivot, front_lower, front_rest, parent_front, relation):
    position = lax.axis_index(("prow", "pcol"))
    leaf = lax.axis_index("leaf")
    spots = lax.axis_size("prow") * lax.axis_size("pcol")
    leaves = lax.axis_size("leaf")
    half_spots = spots // 2
    side = leaf % 2
    partner = leaf + 1 - 2 * side
    pivot_rows = front_pivot[0]
    lower_rows = front_lower[0]
    rest_rows = front_rest[0]
    base = parent_front[0]
    rows_here, child_order = rest_rows.shape
    half = child_order // 2
    height, parent_half = base.shape
    steps = 8
    wide = half // steps
    window = parent_half // steps

    matrix = gather_rows(pivot_rows, spots)

    low_bits = lower_rows.astype(bf16)
    swap = []
    mirror = []
    for one in range(leaves):
        for spot in range(spots):
            mirror.append((one * spots + spot, (one ^ 1) * spots + spot))
            if spot // half_spots != one % 2:
                swap.append((one * spots + spot, (one ^ 1) * spots + (spot ^ half_spots)))
    swapped = lax.ppermute(low_bits, AXES, swap)
    swapped, matrix = lax.optimization_barrier((swapped, matrix))
    block = jnp.where(position // half_spots == side, low_bits, swapped)
    b_all = lax.all_gather(block, ("prow", "pcol"), axis=0, tiled=True)
    other = lax.dynamic_slice_in_dim(rest_rows, (1 - side) * half, half, 1).astype(bf16)
    other, matrix = lax.optimization_barrier((other, matrix))
    rest_sib = lax.ppermute(other, AXES, mirror)

    where = jnp.full((1,), position, jnp.int32)
    pivot_out, lower_out, g = factor(where, matrix, lower_rows, pivot_rows.shape[0])
    g_sib = lax.ppermute(g, AXES, mirror)

    def links(child):
        link = lax.dynamic_index_in_dim(relation, child, 0, keepdims=False)
        row_link = lax.dynamic_slice_in_dim(link, position * rows_here, rows_here, 0) - position * height
        col_link = lax.dynamic_slice_in_dim(link, side * half, half, 0) - side * parent_half
        col_link = col_link.reshape(steps, 1, wide) - jnp.arange(steps, dtype=jnp.int32)[:, None, None] * window
        return row_link[None], col_link

    row_own, col_own = links(leaf)
    row_sib, col_sib = links(partner)
    pick_own = jnp.stack([side * steps, side * steps]).astype(jnp.int32)
    pick_sib = jnp.stack([(1 - side) * steps, 0 * side]).astype(jnp.int32)
    merged = assemble(pick_own, g, b_all, rest_rows, row_own, col_own, base)
    merged = assemble(pick_sib, g_sib, b_all, rest_sib, row_sib, col_sib, merged)
    return (pivot_out[None], lower_out[None], merged[None])


def solution(mesh):
    spec = P("leaf", ("prow", "pcol"), None)
    return jax.shard_map(
        local,
        mesh=mesh,
        in_specs=(spec, spec, spec, spec, P()),
        out_specs=(spec, spec, spec),
        check_vma=False,
    )
```

```python
import functools

import jax
import jax.numpy as jnp
from jax import lax
from jax.experimental import pallas as pl
from jax.experimental.pallas import tpu as pltpu
from jax.sharding import PartitionSpec as P

DB = 128
PB = 256
f32 = jnp.float32
bf16 = jnp.bfloat16


def two_terms(value):
    high = value.astype(bf16)
    low = (value - high.astype(f32)).astype(bf16)
    return high, low


def nt(a, b):
    return lax.dot_general(a, b, (((1,), (1,)), ((), ())), preferred_element_type=f32)


def nn(a, b):
    return lax.dot_general(a, b, (((1,), (0,)), ((), ())), preferred_element_type=f32)


def left3(value):
    high, low = two_terms(value)
    return jnp.concatenate([high, high, low], axis=1)


def right3(value, axis=1):
    high, low = two_terms(value)
    return jnp.concatenate([high, low, high], axis=axis)


def nt3(a, b):
    return nt(left3(a), right3(b))


def nn3(a, b):
    return nn(left3(a), right3(b, 0))


def factor_corner(work, keep, segments=2):
    count = DB // 8
    sub = lax.broadcasted_iota(jnp.int32, (8, DB), 0)

    def wide(row):
        return jnp.broadcast_to(row, (8, DB))

    def step(first, block, carry):
        start = pl.multiple_of(block * 8, 8)
        after = pl.multiple_of(start + 8, 8)
        before = pl.multiple_of(jnp.maximum(start - 8, 0), 8)
        started = jnp.where(block > 0, 1.0, 0.0).astype(f32)
        halves = (slice(0, DB), slice(DB, 2 * DB))
        rows = [work[pl.ds(start, 8), h] for h in halves]
        tile = [work[pl.ds(after, 8), h] for h in halves]
        past = [keep[pl.ds(before, 8), h] for h in halves]
        lane = jnp.zeros((8, DB), jnp.int32) + start
        lane_before = jnp.zeros((8, DB), jnp.int32) + before

        low = (first + 1) * 8
        if low < DB:
            left = work[low:DB, :DB]
            place = lax.broadcasted_iota(jnp.int32, left.shape, 1)
            depth = lax.broadcasted_iota(jnp.int32, left.shape, 0) + low
            chosen = (place >= start - 8) & (place < start) & (depth >= start + 16)
            left = jnp.where(chosen, left, 0.0)
            change = nn3(left, keep[...])

        for k in range(8):
            coef = jnp.take_along_axis(tile[0], lane_before + k, axis=1) * started
            if k == 0:
                drop = [coef * wide(past[s][k:k + 1]) for s in range(2)]
            else:
                drop = [drop[s] + coef * wide(past[s][k:k + 1]) for s in range(2)]
        tile = [tile[s] - drop[s] for s in range(2)]

        a = {}
        side_col = []
        for k in range(8):
            piece = jnp.take_along_axis(rows[0], lane + k, axis=1)
            for s in range(k, 8):
                a[s, k] = wide(piece[s:s + 1])
            side_col.append(jnp.take_along_axis(tile[0], lane + k, axis=1))
        r = []
        up = []
        for i in range(8):
            inv = lax.rsqrt(a[i, i])
            r.append(inv)
            for k in range(i + 1, 8):
                a[k, i] = a[k, i] * inv
            for k in range(i + 1, 8):
                for j in range(i + 1, k + 1):
                    a[k, j] = a[k, j] - a[k, i] * a[j, i]
            side_col[i] = side_col[i] * inv
            for k in range(i + 1, 8):
                side_col[k] = side_col[k] - a[k, i] * side_col[i]
            if i == 0:
                run = [[wide(rows[s][k:k + 1]) for k in range(8)] for s in range(2)]
            pair = []
            for s in range(2):
                value = run[s][i] * inv
                pair.append(value)
                for k in range(i + 1, 8):
                    run[s][k] = run[s][k] - a[k, i] * value
                tile[s] = tile[s] - side_col[i] * value
            up.append(pair)
        if low < DB:
            work[low:DB, :] = work[low:DB, :] - change
        for s in range(2):
            work[pl.ds(after, 8), halves[s]] = tile[s]
            value = up[0][s]
            for i in range(1, 8):
                value = jnp.where(sub == i, up[i][s], value)
            work[pl.ds(start, 8), halves[s]] = value
        back = [None] * 8
        for i in reversed(range(8)):
            pair = []
            for s in range(2):
                value = up[i][s]
                for k in range(i + 1, 8):
                    value = value - a[k, i] * back[k][s]
                pair.append(value * r[i])
            back[i] = pair
        for s in range(2):
            value = back[0][s]
            for i in range(1, 8):
                value = jnp.where(sub == i, back[i][s], value)
            keep[pl.ds(start, 8), halves[s]] = value
        return carry

    size = count // segments
    for seg in range(segments):
        lax.fori_loop(seg * size, (seg + 1) * size, lambda b, c, f=seg * size: step(f, b, c), 0)


MESH = pl.DeviceIdType.MESH


def gather_pivots(own_ref, out_ref, send, local_sem, recv_f, recv_s, recv_c):
    rows = own_ref.shape[0]
    part = rows // 2
    leaf = lax.axis_index("leaf")
    z = lax.axis_index("prow")
    pcol = lax.axis_index("pcol")
    size = 4
    x = pcol // 2
    core = pcol % 2
    flip = core == 1
    f = jnp.where(flip, z, x)
    s = jnp.where(flip, x, z)

    def device(fi, si, ci):
        zi = jnp.where(flip, fi, si)
        xi = jnp.where(flip, si, fi)
        return (leaf, zi, xi * 2 + ci)

    def first(fi, si):
        zi = jnp.where(flip, fi, si)
        xi = jnp.where(flip, si, fi)
        return (zi * 2 * size + xi * 2 + core) * rows

    def window(fi, si, piece):
        top = first(fi, si)
        if piece is None:
            return out_ref.at[pl.ds(pl.multiple_of(top, 8), rows), :]
        return out_ref.at[pl.ds(pl.multiple_of(top + piece * part, 8), part), :]

    def near(v, d):
        return (v + d + size) % size

    f_dev = [device(near(f, 1), s, core), device(near(f, -1), s, core)]
    s_dev = [device(f, near(s, 1), core), device(f, near(s, -1), core)]
    twin = device(f, s, 1 - core)

    barrier = pltpu.get_barrier_semaphore()
    for dev in f_dev + s_dev + [twin]:
        pl.semaphore_signal(barrier, inc=1, device_id=dev, device_id_type=MESH)
    pl.semaphore_wait(barrier, 5)

    started = []

    def push(src, dst, recv_sem, dev):
        copy = pltpu.make_async_remote_copy(
            src_ref=src, dst_ref=dst, send_sem=send.at[len(started)], recv_sem=recv_sem,
            device_id=dev, device_id_type=MESH,
        )
        copy.start()
        started.append(copy)

    def arrived(dst, recv_sem):
        pltpu.make_async_remote_copy(
            src_ref=dst, dst_ref=dst, send_sem=send.at[0], recv_sem=recv_sem,
            device_id=twin, device_id_type=MESH,
        ).wait_recv()

    offsets = [0, -1, 1, 2]

    def pass_on(k, src, fi):
        dst = window(fi, s, None)
        for d in range(2):
            push(src, dst, recv_s.at[k, d], s_dev[d])
        push(src, dst, recv_c.at[0, k], twin)

    own_dst = window(f, s, None)
    for d in range(2):
        push(own_ref, own_dst, recv_f.at[d], f_dev[d])
    pass_on(0, own_ref, f)
    keep = pltpu.make_async_copy(own_ref, own_dst, local_sem)
    keep.start()

    for d, off in ((0, -1), (1, 1)):
        fi = near(f, off)
        arrived(window(fi, s, None), recv_f.at[d])
        push(window(fi, s, d), window(fi, s, d), recv_f.at[2 + d], f_dev[d])
        pass_on(1 + d, window(fi, s, None), fi)

    def second(k):
        fi = near(f, offsets[k])
        for d, off in ((0, -1), (1, 1)):
            si = near(s, off)
            arrived(window(fi, si, None), recv_s.at[k, d])
            push(window(fi, si, d), window(fi, si, d), recv_s.at[k, 2 + d], s_dev[d])
            push(window(fi, si, None), window(fi, si, None), recv_c.at[1 + d, k], twin)

    def third(k):
        fi = near(f, offsets[k])
        si = near(s, 2)
        for d in range(2):
            arrived(window(fi, si, d), recv_s.at[k, 2 + d])
        push(window(fi, si, None), window(fi, si, None), recv_c.at[3, k], twin)

    second(0)
    fi = near(f, 2)
    for d in range(2):
        arrived(window(fi, s, d), recv_f.at[2 + d])
    pass_on(3, window(fi, s, None), fi)
    second(1)
    third(0)
    second(2)
    third(1)
    second(3)
    third(2)
    third(3)

    def twin_window(a, b):
        tf, ts = s, f
        fi = near(tf, offsets[b])
        si = near(ts, (0, -1, 1, 2)[a])
        zi = jnp.where(flip, si, fi)
        xi = jnp.where(flip, fi, si)
        top = (zi * 2 * size + xi * 2 + (1 - core)) * rows
        return out_ref.at[pl.ds(pl.multiple_of(top, 8), rows), :]

    for a in range(4):
        for b in range(4):
            arrived(twin_window(a, b), recv_c.at[a, b])
    for copy in started:
        copy.wait_send()
    keep.wait()


def factor_kernel(order, rows, a_ref, b_ref, l_ref, x_ref, g_ref, m, work, keep, inv, p_hi, p_lo, send, local_sem, recv_f, recv_s, recv_c):
    total = order + rows
    eye = (lax.broadcasted_iota(jnp.int32, (DB, DB), 0) == lax.broadcasted_iota(jnp.int32, (DB, DB), 1)).astype(f32)
    low_mask = lax.broadcasted_iota(jnp.int32, (DB, DB), 0) >= lax.broadcasted_iota(jnp.int32, (DB, DB), 1)
    m[order:, :] = b_ref[...]
    zero = jnp.zeros((DB, DB), f32)
    keep[...] = jnp.zeros_like(keep)
    work[DB:, :] = jnp.zeros((8, 2 * DB), f32)
    gather_pivots(a_ref, m, send, local_sem, recv_f, recv_s, recv_c)
    for p in range(order // PB):
        c0 = p * PB
        c1 = c0 + DB
        c2 = c0 + PB
        work[:DB, :DB] = m[c0:c1, c0:c1]
        work[:DB, DB:] = eye
        factor_corner(work, keep)
        l11 = jnp.where(low_mask, work[:DB, :DB].T, 0.0)
        i11 = work[:DB, DB:]
        l21 = nt3(m[c1:c2, c0:c1], i11)
        work[:DB, :DB] = m[c1:c2, c1:c2] - nt3(l21, l21)
        work[:DB, DB:] = eye
        factor_corner(work, keep)
        l22 = jnp.where(low_mask, work[:DB, :DB].T, 0.0)
        i22 = work[:DB, DB:]
        i21 = -nn3(i22, nn3(l21, i11))
        m[c0:c1, c0:c1] = l11
        m[c0:c1, c1:c2] = zero
        m[c1:c2, c0:c1] = l21
        m[c1:c2, c1:c2] = l22
        inv[c0:c1, :DB] = i11
        inv[c0:c1, DB:] = zero
        inv[c1:c2, :DB] = i21
        inv[c1:c2, DB:] = i22
        panel = nt3(m[c2:, c0:c2], inv[c0:c2, :])
        m[c2:, c0:c2] = panel
        hi, lo = two_terms(panel)
        p_hi[c2:, :] = hi
        p_lo[c2:, :] = lo
        for j in range(c2, order, PB):
            right = jnp.concatenate([p_hi[j:j + PB], p_lo[j:j + PB], p_hi[j:j + PB]], axis=1)
            left = jnp.concatenate([p_hi[j:], p_hi[j:], p_lo[j:]], axis=1)
            m[j:, j:j + PB] = m[j:, j:j + PB] - nt(left, right)
    x_ref[...] = m[order:, :]
    held = l_ref.shape[0]
    top = pl.multiple_of(lax.axis_index(("prow", "pcol")) * held, 8)
    own = m[pl.ds(top, held), :]
    row_id = lax.broadcasted_iota(jnp.int32, own.shape, 0) + top
    col_id = lax.broadcasted_iota(jnp.int32, own.shape, 1)
    l_ref[...] = jnp.where(col_id <= row_id, own, 0.0)
    for p in reversed(range(order // PB)):
        c0 = p * PB
        c2 = c0 + PB
        rhs = m[order:, c0:c2]
        if c2 < order:
            rhs = rhs - nn3(m[order:, c2:], m[c2:order, c0:c2])
        g = nn3(rhs, inv[c0:c2, :])
        m[order:, c0:c2] = g
        g_ref[:, c0:c2] = g.astype(bf16)


def factor(a, b, held):
    order = a.shape[1]
    rows = b.shape[0]
    vm = pl.BlockSpec(memory_space=pltpu.VMEM)
    return pl.pallas_call(
        functools.partial(factor_kernel, order, rows),
        out_shape=(
            jax.ShapeDtypeStruct((held, order), f32),
            jax.ShapeDtypeStruct((rows, order), f32),
            jax.ShapeDtypeStruct((rows, order), bf16),
        ),
        in_specs=[pl.BlockSpec(memory_space=pl.ANY), vm],
        out_specs=(vm, vm, vm),
        scratch_shapes=[
            pltpu.VMEM((order + rows, order), f32),
            pltpu.VMEM((DB + 8, 2 * DB), f32),
            pltpu.VMEM((DB, 2 * DB), f32),
            pltpu.VMEM((order, PB), f32),
            pltpu.VMEM((order + rows, PB), bf16),
            pltpu.VMEM((order + rows, PB), bf16),
            pltpu.SemaphoreType.DMA((40,)),
            pltpu.SemaphoreType.DMA,
            pltpu.SemaphoreType.DMA((4,)),
            pltpu.SemaphoreType.DMA((4, 4)),
            pltpu.SemaphoreType.DMA((4, 4)),
        ],
        compiler_params=pltpu.CompilerParams(
            vmem_limit_bytes=60 * 2**20, collective_id=0, has_side_effects=True
        ),
        cost_estimate=pl.CostEstimate(flops=70 * 10**9, bytes_accessed=2 * 10**7, transcendentals=0),
        name="factor",
    )(a, b)


def assemble_kernel(pick, g_ref, b_ref, c_ref, rows_ref, cols_ref, base_ref, out_ref):
    height = base_ref.shape[0]
    width = base_ref.shape[1]
    schur = c_ref[...].astype(f32) - nt(g_ref[...], b_ref[...])
    high, low = two_terms(schur)
    spot = lax.broadcasted_iota(jnp.int32, (width, high.shape[1]), 0)
    col_table = (spot == cols_ref[0]).astype(bf16)
    spot = lax.broadcasted_iota(jnp.int32, (height, high.shape[0]), 0)
    row_table = (spot == rows_ref[...]).astype(bf16)
    high = nt(high, col_table).astype(bf16)
    low = nt(low, col_table).astype(bf16)
    out_ref[...] = base_ref[...] + (nn(row_table, high) + nn(row_table, low))


def assemble(pick, g, b_all, c, row_link, col_link, base, reuse):
    steps, _, wide = col_link.shape
    rows, order = g.shape
    height, full = base.shape
    window = full // steps
    return pl.pallas_call(
        assemble_kernel,
        out_shape=jax.ShapeDtypeStruct(base.shape, f32),
        grid_spec=pltpu.PrefetchScalarGridSpec(
            num_scalar_prefetch=1,
            grid=(steps,),
            in_specs=[
                pl.BlockSpec((rows, order), lambda t, pick: (0, 0)),
                pl.BlockSpec((wide, order), lambda t, pick: (pick[0] + t, 0)),
                pl.BlockSpec((rows, wide), lambda t, pick: (0, pick[1] + t)),
                pl.BlockSpec((1, rows), lambda t, pick: (0, 0)),
                pl.BlockSpec((1, 1, wide), lambda t, pick: (t, 0, 0)),
                pl.BlockSpec((height, window), lambda t, pick: (0, t)),
            ],
            out_specs=pl.BlockSpec((height, window), lambda t, pick: (0, t)),
        ),
        input_output_aliases={6: 0} if reuse else {},
        cost_estimate=pl.CostEstimate(flops=5 * 10**9, bytes_accessed=2 * 10**7, transcendentals=0),
        name="assemble",
    )(pick, g, b_all, c, row_link, col_link, base)


AXES = ("leaf", "prow", "pcol")


def local(front_pivot, front_lower, front_rest, parent_front, relation):
    position = lax.axis_index(("prow", "pcol"))
    leaf = lax.axis_index("leaf")
    spots = lax.axis_size("prow") * lax.axis_size("pcol")
    leaves = lax.axis_size("leaf")
    half_spots = spots // 2
    side = leaf % 2
    partner = leaf + 1 - 2 * side
    pivot_rows = front_pivot[0]
    lower_rows = front_lower[0]
    rest_rows = front_rest[0]
    base = parent_front[0]
    rows_here, child_order = rest_rows.shape
    half = child_order // 2
    height, parent_half = base.shape
    steps = 8
    wide = half // steps
    window = parent_half // steps


    low_bits = lower_rows.astype(bf16)
    swap = []
    mirror = []
    for one in range(leaves):
        for spot in range(spots):
            mirror.append((one * spots + spot, (one ^ 1) * spots + spot))
            if spot // half_spots != one % 2:
                swap.append((one * spots + spot, (one ^ 1) * spots + (spot ^ half_spots)))
    swapped = lax.ppermute(low_bits, AXES, swap)
    block = jnp.where(position // half_spots == side, low_bits, swapped)
    b_all = lax.all_gather(block, ("prow", "pcol"), axis=0, tiled=True)
    other = lax.dynamic_slice_in_dim(rest_rows, (1 - side) * half, half, 1).astype(bf16)
    rest_sib = lax.ppermute(other, AXES, mirror)

    pivot_out, lower_out, g = factor(pivot_rows, lower_rows, pivot_rows.shape[0])
    g_sib = lax.ppermute(g, AXES, mirror)

    def links(child):
        link = lax.dynamic_index_in_dim(relation, child, 0, keepdims=False)
        row_link = lax.dynamic_slice_in_dim(link, position * rows_here, rows_here, 0) - position * height
        col_link = lax.dynamic_slice_in_dim(link, side * half, half, 0) - side * parent_half
        col_link = col_link.reshape(steps, 1, wide) - jnp.arange(steps, dtype=jnp.int32)[:, None, None] * window
        return row_link[None], col_link

    row_own, col_own = links(leaf)
    row_sib, col_sib = links(partner)
    pick_own = jnp.stack([side * steps, side * steps]).astype(jnp.int32)
    pick_sib = jnp.stack([(1 - side) * steps, 0 * side]).astype(jnp.int32)
    merged = assemble(pick_own, g, b_all, rest_rows, row_own, col_own, base, False)
    merged = assemble(pick_sib, g_sib, b_all, rest_sib, row_sib, col_sib, merged, True)
    return (pivot_out[None], lower_out[None], merged[None])


def solution(mesh):
    spec = P("leaf", ("prow", "pcol"), None)
    return jax.shard_map(
        local,
        mesh=mesh,
        in_specs=(spec, spec, spec, spec, P()),
        out_specs=(spec, spec, spec),
        check_vma=False,
    )
```

```python
import functools

import jax
import jax.numpy as jnp
from jax import lax
from jax.experimental import pallas as pl
from jax.experimental.pallas import tpu as pltpu
from jax.sharding import PartitionSpec as P

DB = 128
PB = 256
f32 = jnp.float32
bf16 = jnp.bfloat16


def two_terms(value):
    high = value.astype(bf16)
    low = (value - high.astype(f32)).astype(bf16)
    return high, low


def nt(a, b):
    return lax.dot_general(a, b, (((1,), (1,)), ((), ())), preferred_element_type=f32)


def nn(a, b):
    return lax.dot_general(a, b, (((1,), (0,)), ((), ())), preferred_element_type=f32)


def left3(value):
    high, low = two_terms(value)
    return jnp.concatenate([high, high, low], axis=1)


def right3(value, axis=1):
    high, low = two_terms(value)
    return jnp.concatenate([high, low, high], axis=axis)


def nt3(a, b):
    return nt(left3(a), right3(b))


def nn3(a, b):
    return nn(left3(a), right3(b, 0))


def factor_corner(work, keep, pause, segments=2):
    count = DB // 8
    sub = lax.broadcasted_iota(jnp.int32, (8, DB), 0)

    def wide(row):
        return jnp.broadcast_to(row, (8, DB))

    def step(first, block, carry):
        start = pl.multiple_of(block * 8, 8)
        after = pl.multiple_of(start + 8, 8)
        before = pl.multiple_of(jnp.maximum(start - 8, 0), 8)
        started = jnp.where(block > 0, 1.0, 0.0).astype(f32)
        halves = (slice(0, DB), slice(DB, 2 * DB))
        rows = [work[pl.ds(start, 8), h] for h in halves]
        tile = [work[pl.ds(after, 8), h] for h in halves]
        past = [keep[pl.ds(before, 8), h] for h in halves]
        lane = jnp.zeros((8, DB), jnp.int32) + start
        lane_before = jnp.zeros((8, DB), jnp.int32) + before

        low = (first + 1) * 8
        if low < DB:
            left = work[low:DB, :DB]
            place = lax.broadcasted_iota(jnp.int32, left.shape, 1)
            depth = lax.broadcasted_iota(jnp.int32, left.shape, 0) + low
            chosen = (place >= start - 8) & (place < start) & (depth >= start + 16)
            left = jnp.where(chosen, left, 0.0)
            change = nn3(left, keep[...])

        for k in range(8):
            coef = jnp.take_along_axis(tile[0], lane_before + k, axis=1) * started
            if k == 0:
                drop = [coef * wide(past[s][k:k + 1]) for s in range(2)]
            else:
                drop = [drop[s] + coef * wide(past[s][k:k + 1]) for s in range(2)]
        tile = [tile[s] - drop[s] for s in range(2)]

        a = {}
        side_col = []
        for k in range(8):
            piece = jnp.take_along_axis(rows[0], lane + k, axis=1)
            for s in range(k, 8):
                a[s, k] = wide(piece[s:s + 1])
            side_col.append(jnp.take_along_axis(tile[0], lane + k, axis=1))
        r = []
        up = []
        for i in range(8):
            inv = lax.rsqrt(a[i, i])
            r.append(inv)
            for k in range(i + 1, 8):
                a[k, i] = a[k, i] * inv
            for k in range(i + 1, 8):
                for j in range(i + 1, k + 1):
                    a[k, j] = a[k, j] - a[k, i] * a[j, i]
            side_col[i] = side_col[i] * inv
            for k in range(i + 1, 8):
                side_col[k] = side_col[k] - a[k, i] * side_col[i]
            if i == 0:
                run = [[wide(rows[s][k:k + 1]) for k in range(8)] for s in range(2)]
            pair = []
            for s in range(2):
                value = run[s][i] * inv
                pair.append(value)
                for k in range(i + 1, 8):
                    run[s][k] = run[s][k] - a[k, i] * value
                tile[s] = tile[s] - side_col[i] * value
            up.append(pair)
        if low < DB:
            work[low:DB, :] = work[low:DB, :] - change
        for s in range(2):
            work[pl.ds(after, 8), halves[s]] = tile[s]
            value = up[0][s]
            for i in range(1, 8):
                value = jnp.where(sub == i, up[i][s], value)
            work[pl.ds(start, 8), halves[s]] = value
        back = [None] * 8
        for i in reversed(range(8)):
            pair = []
            for s in range(2):
                value = up[i][s]
                for k in range(i + 1, 8):
                    value = value - a[k, i] * back[k][s]
                pair.append(value * r[i])
            back[i] = pair
        for s in range(2):
            value = back[0][s]
            for i in range(1, 8):
                value = jnp.where(sub == i, back[i][s], value)
            keep[pl.ds(start, 8), halves[s]] = value
        return carry

    size = count // segments
    for seg in range(segments):
        lax.fori_loop(seg * size, (seg + 1) * size, lambda b, c, f=seg * size: step(f, b, c), 0)
        pause()


MESH = pl.DeviceIdType.MESH
RING = 4


class Place:
    def __init__(self):
        self.leaf = lax.axis_index("leaf")
        self.z = lax.axis_index("prow")
        pcol = lax.axis_index("pcol")
        self.x = pcol // 2
        self.core = pcol % 2
        self.flip = self.core == 1
        self.f = jnp.where(self.flip, self.z, self.x)
        self.s = jnp.where(self.flip, self.x, self.z)
        self.f_dev = [self.device(self.near(self.f, 1), self.s), self.device(self.near(self.f, -1), self.s)]
        self.s_dev = [self.device(self.f, self.near(self.s, 1)), self.device(self.f, self.near(self.s, -1))]
        self.twin = (self.leaf, self.z, self.x * 2 + 1 - self.core)
        self.far_dev = [self.device(self.near(self.f, 2), self.s), self.device(self.f, self.near(self.s, 2))]

    def near(self, v, d):
        return (v + d + RING) % RING

    def chip(self, fi, si):
        return jnp.where(self.flip, fi, si), jnp.where(self.flip, si, fi)

    def device(self, fi, si):
        zi, xi = self.chip(fi, si)
        return (self.leaf, zi, xi * 2 + self.core)


class Gather:
    OFFSETS = (0, -1, 1, 2)

    def __init__(self, place, source, view, rows, send, recv, needed=None, direct=False):
        self.place = place
        self.source = source
        self.view = view
        self.rows = rows
        self.send = send
        self.recv = recv
        self.needed = needed
        self.direct = direct
        self.started = []

    def window(self, fi, si, piece=None, twin=False):
        p = self.place
        zi, xi = p.chip(fi, si)
        slot = zi * 2 * RING + xi * 2 + ((1 - p.core) if twin else p.core)
        top = slot * self.rows
        part = self.rows // 2
        if piece is None:
            return self.view(pl.multiple_of(top, 8), self.rows)
        return self.view(pl.multiple_of(top + piece * part, 8), part)

    def under(self, fi, si, action):
        if self.needed is None:
            action()
        else:
            pl.when(self.needed(self.place.chip(fi, si)[0]))(action)

    def push(self, fi, si, src, dst, sem, dev):
        copy = pltpu.make_async_remote_copy(
            src_ref=src, dst_ref=dst, send_sem=self.send.at[len(self.started)],
            recv_sem=self.recv.at[sem], device_id=dev, device_id_type=MESH,
        )
        self.started.append((fi, si, copy))
        self.under(fi, si, copy.start)

    def arrived(self, fi, si, dst, sem):
        copy = pltpu.make_async_remote_copy(
            src_ref=dst, dst_ref=dst, send_sem=self.send.at[0],
            recv_sem=self.recv.at[sem], device_id=self.place.twin, device_id_type=MESH,
        )
        self.under(fi, si, copy.wait_recv)

    def f_sem(self, d):
        return d

    def s_sem(self, k, d):
        return 4 + 4 * k + d

    def c_sem(self, a, k):
        return 20 + 4 * a + k

    def pass_on(self, k, src, fi):
        p = self.place
        dst = self.window(fi, p.s)
        for d in range(2):
            self.push(fi, p.s, src, dst, self.s_sem(k, d), p.s_dev[d])
        if self.direct:
            self.push(fi, p.s, src, dst, self.s_sem(k, 2), p.far_dev[1])
        self.push(fi, p.s, src, dst, self.c_sem(0, k), p.twin)

    def begin(self):
        p = self.place
        for d in range(2):
            self.push(p.f, p.s, self.source, self.window(p.f, p.s), self.f_sem(d), p.f_dev[d])
        if self.direct:
            self.push(p.f, p.s, self.source, self.window(p.f, p.s), self.f_sem(2), p.far_dev[0])
        self.pass_on(0, self.source, p.f)

    def sides(self):
        p = self.place
        for d, off in ((0, -1), (1, 1)):
            fi = p.near(p.f, off)
            self.arrived(fi, p.s, self.window(fi, p.s), self.f_sem(d))
            if not self.direct:
                half = self.window(fi, p.s, d)
                self.push(fi, p.s, half, half, self.f_sem(2 + d), p.f_dev[d])
            self.pass_on(1 + d, self.window(fi, p.s), fi)

    def far(self):
        p = self.place
        fi = p.near(p.f, 2)
        if self.direct:
            self.arrived(fi, p.s, self.window(fi, p.s), self.f_sem(2))
        else:
            for d in range(2):
                self.arrived(fi, p.s, self.window(fi, p.s, d), self.f_sem(2 + d))
        self.pass_on(3, self.window(fi, p.s), fi)

    def second(self, k):
        p = self.place
        fi = p.near(p.f, self.OFFSETS[k])
        for d, off in ((0, -1), (1, 1)):
            si = p.near(p.s, off)
            self.arrived(fi, si, self.window(fi, si), self.s_sem(k, d))
            if not self.direct:
                half = self.window(fi, si, d)
                self.push(fi, si, half, half, self.s_sem(k, 2 + d), p.s_dev[d])
            whole = self.window(fi, si)
            self.push(fi, si, whole, whole, self.c_sem(1 + d, k), p.twin)

    def third(self, k):
        p = self.place
        fi = p.near(p.f, self.OFFSETS[k])
        si = p.near(p.s, 2)
        if self.direct:
            self.arrived(fi, si, self.window(fi, si), self.s_sem(k, 2))
        else:
            for d in range(2):
                self.arrived(fi, si, self.window(fi, si, d), self.s_sem(k, 2 + d))
        whole = self.window(fi, si)
        self.push(fi, si, whole, whole, self.c_sem(3, k), p.twin)

    def close(self):
        p = self.place
        for a in range(4):
            for b in range(4):
                fi = p.near(p.f, self.OFFSETS[a])
                si = p.near(p.s, self.OFFSETS[b])
                self.arrived(fi, si, self.window(fi, si, twin=True), self.c_sem(a, b))
        for fi, si, copy in self.started:
            self.under(fi, si, copy.wait_send)


CUTS = (0, 256, 512, 1024, 1536)


def factor_kernel(
    order, rows, a_ref, b_ref, l_ref, x_ref, g_ref,
    m, work, keep, inv, p_hi, p_lo, send, recv, extra,
):
    place = Place()
    held = l_ref.shape[0]
    eye = (lax.broadcasted_iota(jnp.int32, (DB, DB), 0) == lax.broadcasted_iota(jnp.int32, (DB, DB), 1)).astype(f32)
    low_mask = lax.broadcasted_iota(jnp.int32, (DB, DB), 0) >= lax.broadcasted_iota(jnp.int32, (DB, DB), 1)
    zero = jnp.zeros((DB, DB), f32)

    spot = place.z * 2 * RING + place.x * 2 + place.core
    own_rows = pl.ds(pl.multiple_of(spot * held, 8), held)

    groups = []
    needs = (None, None, lambda zi: zi >= 1, lambda zi: zi >= 2)
    for n in range(4):
        cols = slice(CUTS[n], CUTS[n + 1])
        groups.append(Gather(
            place, a_ref.at[:, cols],
            lambda top, size, cols=cols: m.at[pl.ds(top, size), cols],
            held, send.at[n], recv.at[n], needs[n], n < 2,
        ))
    mine = pltpu.make_async_copy(a_ref, m.at[own_rows, :], extra)

    barrier = pltpu.get_barrier_semaphore()
    peers = place.f_dev + place.s_dev + place.far_dev + [place.twin]
    for dev in peers:
        pl.semaphore_signal(barrier, inc=1, device_id=dev, device_id_type=MESH)
    mine.start()
    pl.semaphore_wait(barrier, len(peers))

    first, mid, late, last = groups
    first.begin()
    m[order:, :] = b_ref[...]
    keep[...] = jnp.zeros_like(keep)
    work[DB:, :] = jnp.zeros((8, 2 * DB), f32)
    first.sides()
    first.far()
    mid.begin()
    first.second(0)
    first.second(1)
    first.second(2)
    first.third(0)
    first.third(1)
    first.second(3)
    first.third(2)
    first.third(3)
    late.begin()
    last.begin()
    first.close()
    mine.wait()

    plan = {
        (0, 0): [mid.sides, mid.far],
        (0, 1): [lambda: mid.second(0), lambda: mid.second(1), lambda: mid.second(2), late.sides],
        (0, 2): [lambda: mid.third(0), lambda: mid.third(1), lambda: mid.second(3), lambda: late.second(0), late.far],
        (0, 3): [lambda: mid.third(2), lambda: mid.third(3), lambda: late.second(1), lambda: late.third(0)],
        (0, 4): [mid.close, last.sides],
        (0, 5): [lambda: late.second(2), lambda: late.third(1)],
        (1, 0): [lambda: late.second(3), lambda: late.third(2), lambda: last.second(0)],
        (1, 1): [lambda: late.third(3), last.far],
        (1, 2): [lambda: last.second(1), lambda: last.third(0)],
        (1, 4): [late.close],
        (1, 5): [lambda: last.second(2), lambda: last.third(1)],
        (2, 1): [lambda: last.second(3), lambda: last.third(2)],
        (2, 3): [lambda: last.third(3)],
        (2, 4): [last.close],
    }

    def update(q, j):
        j2 = j + PB
        qs = slice(q * PB, q * PB + PB)
        right = jnp.concatenate([p_hi[j:j2, qs], p_lo[j:j2, qs], p_hi[j:j2, qs]], axis=1)
        left = jnp.concatenate([p_hi[j:, qs], p_hi[j:, qs], p_lo[j:, qs]], axis=1)
        m[j:, j:j2] = m[j:, j:j2] - nt(left, right)

    for p in range(order // PB):
        count = [0]

        def pause():
            for action in plan.get((p, count[0]), ()):
                action()
            count[0] += 1

        c0 = p * PB
        c1 = c0 + DB
        c2 = c0 + PB
        work[:DB, :DB] = m[c0:c1, c0:c1]
        work[:DB, DB:] = eye
        factor_corner(work, keep, pause)
        l11 = jnp.where(low_mask, work[:DB, :DB].T, 0.0)
        i11 = work[:DB, DB:]
        l21 = nt3(m[c1:c2, c0:c1], i11)
        work[:DB, :DB] = m[c1:c2, c1:c2] - nt3(l21, l21)
        work[:DB, DB:] = eye
        m[c0:c1, c0:c1] = l11
        m[c0:c1, c1:c2] = zero
        m[c1:c2, c0:c1] = l21
        inv[c0:c1, :DB] = i11
        inv[c0:c1, DB:] = zero
        factor_corner(work, keep, pause)
        l22 = jnp.where(low_mask, work[:DB, :DB].T, 0.0)
        i22 = work[:DB, DB:]
        i21 = -nn3(i22, nn3(m[c1:c2, c0:c1], inv[c0:c1, :DB]))
        m[c1:c2, c1:c2] = l22
        inv[c1:c2, :DB] = i21
        inv[c1:c2, DB:] = i22
        panel = nt3(m[c2:, c0:c2], inv[c0:c2, :])
        m[c2:, c0:c2] = panel
        hi, lo = two_terms(panel)
        p_hi[c2:, c0:c2] = hi
        p_lo[c2:, c0:c2] = lo
        pause()
        for j in range(c2, order, PB):
            opens = max(CUTS[n] for n in range(4) if CUTS[n] <= j)
            due = {256: 0, 512: 1, 1024: 2}[opens]
            if p == due:
                for q in range(p):
                    update(q, j)
            if p >= due:
                update(p, j)
        pause()
    x_ref[...] = m[order:, :]
    own = m[own_rows, :]
    row_id = lax.broadcasted_iota(jnp.int32, own.shape, 0) + spot * held
    col_id = lax.broadcasted_iota(jnp.int32, own.shape, 1)
    l_ref[...] = jnp.where(col_id <= row_id, own, 0.0)
    for p in reversed(range(order // PB)):
        c0 = p * PB
        c2 = c0 + PB
        rhs = m[order:, c0:c2]
        if c2 < order:
            rhs = rhs - nn3(m[order:, c2:], m[c2:order, c0:c2])
        g = nn3(rhs, inv[c0:c2, :])
        m[order:, c0:c2] = g
        g_ref[:, c0:c2] = g.astype(bf16)


def factor(a, b):
    held, order = a.shape
    rows = b.shape[0]
    vm = pl.BlockSpec(memory_space=pltpu.VMEM)
    return pl.pallas_call(
        functools.partial(factor_kernel, order, rows),
        out_shape=(
            jax.ShapeDtypeStruct((held, order), f32),
            jax.ShapeDtypeStruct((rows, order), f32),
            jax.ShapeDtypeStruct((rows, order), bf16),
        ),
        in_specs=[vm, vm],
        out_specs=(vm, vm, vm),
        scratch_shapes=[
            pltpu.VMEM((order + rows, order), f32),
            pltpu.VMEM((DB + 8, 2 * DB), f32),
            pltpu.VMEM((DB, 2 * DB), f32),
            pltpu.VMEM((order, PB), f32),
            pltpu.VMEM((order + rows, order), bf16),
            pltpu.VMEM((order + rows, order), bf16),
            pltpu.SemaphoreType.DMA((4, 36)),
            pltpu.SemaphoreType.DMA((4, 36)),
            pltpu.SemaphoreType.DMA,
        ],
        compiler_params=pltpu.CompilerParams(
            vmem_limit_bytes=60 * 2**20, collective_id=0, has_side_effects=True
        ),
        cost_estimate=pl.CostEstimate(flops=100 * 10**9, bytes_accessed=2 * 10**7, transcendentals=0),
        name="factor",
    )(a, b)


def tables(rows_ref, cols_ref, height, width):
    rows = rows_ref.shape[1]
    cols = cols_ref.shape[2]
    row_table = (lax.broadcasted_iota(jnp.int32, (height, rows), 0) == rows_ref[...]).astype(bf16)
    col_table = (lax.broadcasted_iota(jnp.int32, (width, cols), 0) == cols_ref[0]).astype(bf16)
    return row_table, col_table


def send_kernel(pick, g_ref, b_ref, c_ref, out_ref):
    out_ref[...] = (c_ref[...] - nt(g_ref[...], b_ref[...])).astype(bf16)


def keep_kernel(pick, g_ref, b_ref, c_ref, rows_ref, cols_ref, base_ref, out_ref):
    row_table, col_table = tables(rows_ref, cols_ref, *base_ref.shape)
    high, low = two_terms(c_ref[...] - nt(g_ref[...], b_ref[...]))
    high = nt(high, col_table).astype(bf16)
    low = nt(low, col_table).astype(bf16)
    out_ref[...] = base_ref[...] + (nn(row_table, high) + nn(row_table, low))


def join_kernel(s_ref, rows_ref, cols_ref, base_ref, out_ref):
    row_table, col_table = tables(rows_ref, cols_ref, *base_ref.shape)
    out_ref[...] = base_ref[...] + nn(row_table, nt(s_ref[...], col_table).astype(bf16))


def cost(flops):
    return pl.CostEstimate(flops=flops, bytes_accessed=10**7, transcendentals=0)


def send_part(pick, g, b_all, c, wide, steps):
    rows, order = g.shape
    return pl.pallas_call(
        send_kernel,
        out_shape=jax.ShapeDtypeStruct((rows, wide * steps), bf16),
        grid_spec=pltpu.PrefetchScalarGridSpec(
            num_scalar_prefetch=1,
            grid=(steps,),
            in_specs=[
                pl.BlockSpec((rows, order), lambda t, pick: (0, 0)),
                pl.BlockSpec((wide, order), lambda t, pick: (pick[0] + t, 0)),
                pl.BlockSpec((rows, wide), lambda t, pick: (0, pick[0] + t)),
            ],
            out_specs=pl.BlockSpec((rows, wide), lambda t, pick: (0, t)),
        ),
        cost_estimate=cost(10**9),
        name="send_part",
    )(pick, g, b_all, c)


def keep_part(pick, g, b_all, c, row_link, col_link, base):
    steps, _, wide = col_link.shape
    rows, order = g.shape
    height, full = base.shape
    window = full // steps
    return pl.pallas_call(
        keep_kernel,
        out_shape=jax.ShapeDtypeStruct(base.shape, f32),
        grid_spec=pltpu.PrefetchScalarGridSpec(
            num_scalar_prefetch=1,
            grid=(steps,),
            in_specs=[
                pl.BlockSpec((rows, order), lambda t, pick: (0, 0)),
                pl.BlockSpec((wide, order), lambda t, pick: (pick[0] + t, 0)),
                pl.BlockSpec((rows, wide), lambda t, pick: (0, pick[0] + t)),
                pl.BlockSpec((1, rows), lambda t, pick: (0, 0)),
                pl.BlockSpec((1, 1, wide), lambda t, pick: (t, 0, 0)),
                pl.BlockSpec((height, window), lambda t, pick: (0, t)),
            ],
            out_specs=pl.BlockSpec((height, window), lambda t, pick: (0, t)),
        ),
        cost_estimate=cost(5 * 10**9),
        name="keep_part",
    )(pick, g, b_all, c, row_link, col_link, base)


def join_part(part, parts, got, row_link, col_link, base):
    steps, _, wide = col_link.shape
    rows = got.shape[0]
    height, full = base.shape
    window = full // steps
    count = steps // parts
    first = part * count
    return pl.pallas_call(
        join_kernel,
        out_shape=jax.ShapeDtypeStruct(base.shape, f32),
        grid=(count,),
        in_specs=[
            pl.BlockSpec((rows, wide), lambda t: (0, t)),
            pl.BlockSpec((1, rows), lambda t: (0, 0)),
            pl.BlockSpec((1, 1, wide), lambda t: (t + first, 0, 0)),
            pl.BlockSpec((height, window), lambda t: (0, t + first)),
        ],
        out_specs=pl.BlockSpec((height, window), lambda t: (0, t + first)),
        input_output_aliases={3: 0},
        cost_estimate=cost(10**9),
        name="join_part",
    )(got, row_link, col_link, base)


AXES = ("leaf", "prow", "pcol")


def local(front_pivot, front_lower, front_rest, parent_front, relation):
    position = lax.axis_index(("prow", "pcol"))
    leaf = lax.axis_index("leaf")
    spots = lax.axis_size("prow") * lax.axis_size("pcol")
    leaves = lax.axis_size("leaf")
    side = leaf % 2
    partner = leaf + 1 - 2 * side
    pivot_rows = front_pivot[0]
    lower_rows = front_lower[0]
    rest_rows = front_rest[0]
    base = parent_front[0]
    rows_here, child_order = rest_rows.shape
    half = child_order // 2
    height, parent_half = base.shape
    steps = 8
    wide = half // steps
    window = parent_half // steps


    mirror = [(one * spots + spot, (one ^ 1) * spots + spot) for one in range(leaves) for spot in range(spots)]
    b_all = lax.all_gather(lower_rows.astype(bf16), ("prow", "pcol"), axis=0, tiled=True)
    pivot_out, lower_out, g = factor(pivot_rows, lower_rows)

    def links(child):
        link = lax.dynamic_index_in_dim(relation, child, 0, keepdims=False)
        row_link = lax.dynamic_slice_in_dim(link, position * rows_here, rows_here, 0) - position * height
        col_link = lax.dynamic_slice_in_dim(link, side * half, half, 0) - side * parent_half
        col_link = col_link.reshape(steps, 1, wide) - jnp.arange(steps, dtype=jnp.int32)[:, None, None] * window
        return row_link[None], col_link

    row_own, col_own = links(leaf)
    row_sib, col_sib = links(partner)
    received = []
    parts = 2
    for part in range(parts):
        pick = jnp.full((1,), (1 - side) * steps + part * (steps // parts), jnp.int32)
        sent = send_part(pick, g, b_all, rest_rows, wide, steps // parts)
        received.append(lax.ppermute(sent, AXES, mirror))
    merged = keep_part(jnp.full((1,), side * steps, jnp.int32), g, b_all, rest_rows, row_own, col_own, base)
    for part in range(parts):
        merged = join_part(part, parts, received[part], row_sib, col_sib, merged)
    return (pivot_out[None], lower_out[None], merged[None])


def solution(mesh):
    spec = P("leaf", ("prow", "pcol"), None)
    return jax.shard_map(
        local,
        mesh=mesh,
        in_specs=(spec, spec, spec, spec, P()),
        out_specs=(spec, spec, spec),
        check_vma=False,
    )
```

```python
import functools

import jax
import jax.numpy as jnp
from jax import lax
from jax.experimental import pallas as pl
from jax.experimental.pallas import tpu as pltpu
from jax.sharding import PartitionSpec as P

DB = 128
PB = 256
f32 = jnp.float32
bf16 = jnp.bfloat16


def two_terms(value):
    high = value.astype(bf16)
    low = (value - high.astype(f32)).astype(bf16)
    return high, low


def nt(a, b):
    return lax.dot_general(a, b, (((1,), (1,)), ((), ())), preferred_element_type=f32)


def nn(a, b):
    return lax.dot_general(a, b, (((1,), (0,)), ((), ())), preferred_element_type=f32)


def left3(value):
    high, low = two_terms(value)
    return jnp.concatenate([high, high, low], axis=1)


def right3(value, axis=1):
    high, low = two_terms(value)
    return jnp.concatenate([high, low, high], axis=axis)


def nt3(a, b):
    return nt(left3(a), right3(b))


def nn3(a, b):
    return nn(left3(a), right3(b, 0))


def factor_corner(work, keep, pause, segments=2):
    count = DB // 8
    sub = lax.broadcasted_iota(jnp.int32, (8, DB), 0)

    def wide(row):
        return jnp.broadcast_to(row, (8, DB))

    def step(first, block, carry):
        start = pl.multiple_of(block * 8, 8)
        after = pl.multiple_of(start + 8, 8)
        before = pl.multiple_of(jnp.maximum(start - 8, 0), 8)
        started = jnp.where(block > 0, 1.0, 0.0).astype(f32)
        halves = (slice(0, DB), slice(DB, 2 * DB))
        rows = [work[pl.ds(start, 8), h] for h in halves]
        tile = [work[pl.ds(after, 8), h] for h in halves]
        past = [keep[pl.ds(before, 8), h] for h in halves]
        lane = jnp.zeros((8, DB), jnp.int32) + start
        lane_before = jnp.zeros((8, DB), jnp.int32) + before

        low = (first + 1) * 8
        if low < DB:
            left = work[low:DB, :DB]
            place = lax.broadcasted_iota(jnp.int32, left.shape, 1)
            depth = lax.broadcasted_iota(jnp.int32, left.shape, 0) + low
            chosen = (place >= start - 8) & (place < start) & (depth >= start + 16)
            left = jnp.where(chosen, left, 0.0)
            change = nn3(left, keep[...])

        for k in range(8):
            coef = jnp.take_along_axis(tile[0], lane_before + k, axis=1) * started
            if k == 0:
                drop = [coef * wide(past[s][k:k + 1]) for s in range(2)]
            else:
                drop = [drop[s] + coef * wide(past[s][k:k + 1]) for s in range(2)]
        tile = [tile[s] - drop[s] for s in range(2)]

        a = {}
        side_col = []
        for k in range(8):
            piece = jnp.take_along_axis(rows[0], lane + k, axis=1)
            for s in range(k, 8):
                a[s, k] = wide(piece[s:s + 1])
            side_col.append(jnp.take_along_axis(tile[0], lane + k, axis=1))
        r = []
        up = []
        for i in range(8):
            inv = lax.rsqrt(a[i, i])
            r.append(inv)
            for k in range(i + 1, 8):
                a[k, i] = a[k, i] * inv
            for k in range(i + 1, 8):
                for j in range(i + 1, k + 1):
                    a[k, j] = a[k, j] - a[k, i] * a[j, i]
            side_col[i] = side_col[i] * inv
            for k in range(i + 1, 8):
                side_col[k] = side_col[k] - a[k, i] * side_col[i]
            if i == 0:
                run = [[wide(rows[s][k:k + 1]) for k in range(8)] for s in range(2)]
            pair = []
            for s in range(2):
                value = run[s][i] * inv
                pair.append(value)
                for k in range(i + 1, 8):
                    run[s][k] = run[s][k] - a[k, i] * value
                tile[s] = tile[s] - side_col[i] * value
            up.append(pair)
        if low < DB:
            work[low:DB, :] = work[low:DB, :] - change
        for s in range(2):
            work[pl.ds(after, 8), halves[s]] = tile[s]
            value = up[0][s]
            for i in range(1, 8):
                value = jnp.where(sub == i, up[i][s], value)
            work[pl.ds(start, 8), halves[s]] = value
        back = [None] * 8
        for i in reversed(range(8)):
            pair = []
            for s in range(2):
                value = up[i][s]
                for k in reversed(range(i + 1, 8)):
                    value = value - a[k, i] * back[k][s]
                pair.append(value * r[i])
            back[i] = pair
        for s in range(2):
            value = back[0][s]
            for i in range(1, 8):
                value = jnp.where(sub == i, back[i][s], value)
            keep[pl.ds(start, 8), halves[s]] = value
        return carry

    size = count // segments
    for seg in range(segments):
        lax.fori_loop(seg * size, (seg + 1) * size, lambda b, c, f=seg * size: step(f, b, c), 0)
        pause()


MESH = pl.DeviceIdType.MESH
RING = 4


class Place:
    def __init__(self):
        self.leaf = lax.axis_index("leaf")
        self.z = lax.axis_index("prow")
        pcol = lax.axis_index("pcol")
        self.x = pcol // 2
        self.core = pcol % 2
        self.flip = self.core == 1
        self.f = jnp.where(self.flip, self.z, self.x)
        self.s = jnp.where(self.flip, self.x, self.z)
        self.f_dev = [self.device(self.near(self.f, 1), self.s), self.device(self.near(self.f, -1), self.s)]
        self.s_dev = [self.device(self.f, self.near(self.s, 1)), self.device(self.f, self.near(self.s, -1))]
        self.twin = (self.leaf, self.z, self.x * 2 + 1 - self.core)
        self.far_dev = [self.device(self.near(self.f, 2), self.s), self.device(self.f, self.near(self.s, 2))]

    def near(self, v, d):
        return (v + d + RING) % RING

    def chip(self, fi, si):
        return jnp.where(self.flip, fi, si), jnp.where(self.flip, si, fi)

    def device(self, fi, si):
        zi, xi = self.chip(fi, si)
        return (self.leaf, zi, xi * 2 + self.core)


class Gather:
    OFFSETS = (0, -1, 1, 2)

    def __init__(self, place, source, view, rows, send, recv, needed=None, direct=False):
        self.place = place
        self.source = source
        self.view = view
        self.rows = rows
        self.send = send
        self.recv = recv
        self.needed = needed
        self.direct = direct
        self.started = []

    def window(self, fi, si, piece=None, twin=False):
        p = self.place
        zi, xi = p.chip(fi, si)
        slot = zi * 2 * RING + xi * 2 + ((1 - p.core) if twin else p.core)
        top = slot * self.rows
        part = self.rows // 2
        if piece is None:
            return self.view(pl.multiple_of(top, 8), self.rows)
        return self.view(pl.multiple_of(top + piece * part, 8), part)

    def under(self, fi, si, action):
        if self.needed is None:
            action()
        else:
            pl.when(self.needed(self.place.chip(fi, si)[0]))(action)

    def push(self, fi, si, src, dst, sem, dev):
        copy = pltpu.make_async_remote_copy(
            src_ref=src, dst_ref=dst, send_sem=self.send.at[len(self.started)],
            recv_sem=self.recv.at[sem], device_id=dev, device_id_type=MESH,
        )
        self.started.append((fi, si, copy))
        self.under(fi, si, copy.start)

    def arrived(self, fi, si, dst, sem):
        copy = pltpu.make_async_remote_copy(
            src_ref=dst, dst_ref=dst, send_sem=self.send.at[0],
            recv_sem=self.recv.at[sem], device_id=self.place.twin, device_id_type=MESH,
        )
        self.under(fi, si, copy.wait_recv)

    def f_sem(self, d):
        return d

    def s_sem(self, k, d):
        return 4 + 4 * k + d

    def c_sem(self, a, k):
        return 20 + 4 * a + k

    def pass_on(self, k, src, fi):
        p = self.place
        dst = self.window(fi, p.s)
        for d in range(2):
            self.push(fi, p.s, src, dst, self.s_sem(k, d), p.s_dev[d])
        if self.direct:
            self.push(fi, p.s, src, dst, self.s_sem(k, 2), p.far_dev[1])
        self.push(fi, p.s, src, dst, self.c_sem(0, k), p.twin)

    def begin(self):
        p = self.place
        for d in range(2):
            self.push(p.f, p.s, self.source, self.window(p.f, p.s), self.f_sem(d), p.f_dev[d])
        if self.direct:
            self.push(p.f, p.s, self.source, self.window(p.f, p.s), self.f_sem(2), p.far_dev[0])
        self.pass_on(0, self.source, p.f)

    def sides(self):
        p = self.place
        for d, off in ((0, -1), (1, 1)):
            fi = p.near(p.f, off)
            self.arrived(fi, p.s, self.window(fi, p.s), self.f_sem(d))
            if not self.direct:
                half = self.window(fi, p.s, d)
                self.push(fi, p.s, half, half, self.f_sem(2 + d), p.f_dev[d])
            self.pass_on(1 + d, self.window(fi, p.s), fi)

    def far(self):
        p = self.place
        fi = p.near(p.f, 2)
        if self.direct:
            self.arrived(fi, p.s, self.window(fi, p.s), self.f_sem(2))
        else:
            for d in range(2):
                self.arrived(fi, p.s, self.window(fi, p.s, d), self.f_sem(2 + d))
        self.pass_on(3, self.window(fi, p.s), fi)

    def second(self, k):
        p = self.place
        fi = p.near(p.f, self.OFFSETS[k])
        for d, off in ((0, -1), (1, 1)):
            si = p.near(p.s, off)
            self.arrived(fi, si, self.window(fi, si), self.s_sem(k, d))
            if not self.direct:
                half = self.window(fi, si, d)
                self.push(fi, si, half, half, self.s_sem(k, 2 + d), p.s_dev[d])
            whole = self.window(fi, si)
            self.push(fi, si, whole, whole, self.c_sem(1 + d, k), p.twin)

    def third(self, k):
        p = self.place
        fi = p.near(p.f, self.OFFSETS[k])
        si = p.near(p.s, 2)
        if self.direct:
            self.arrived(fi, si, self.window(fi, si), self.s_sem(k, 2))
        else:
            for d in range(2):
                self.arrived(fi, si, self.window(fi, si, d), self.s_sem(k, 2 + d))
        whole = self.window(fi, si)
        self.push(fi, si, whole, whole, self.c_sem(3, k), p.twin)

    def close(self):
        p = self.place
        for a in range(4):
            for b in range(4):
                fi = p.near(p.f, self.OFFSETS[a])
                si = p.near(p.s, self.OFFSETS[b])
                self.arrived(fi, si, self.window(fi, si, twin=True), self.c_sem(a, b))
        for fi, si, copy in self.started:
            self.under(fi, si, copy.wait_send)


CUTS = (0, 256, 512, 1024, 1536)


def factor_kernel(
    order, rows, a_ref, b_ref, l_ref, x_ref, g_ref,
    m, work, keep, inv, p_hi, p_lo, send, recv, extra,
):
    place = Place()
    held = l_ref.shape[0]
    eye = (lax.broadcasted_iota(jnp.int32, (DB, DB), 0) == lax.broadcasted_iota(jnp.int32, (DB, DB), 1)).astype(f32)
    low_mask = lax.broadcasted_iota(jnp.int32, (DB, DB), 0) >= lax.broadcasted_iota(jnp.int32, (DB, DB), 1)
    zero = jnp.zeros((DB, DB), f32)

    spot = place.z * 2 * RING + place.x * 2 + place.core
    own_rows = pl.ds(pl.multiple_of(spot * held, 8), held)

    groups = []
    needs = (None, None, lambda zi: zi >= 1, lambda zi: zi >= 2)
    for n in range(4):
        cols = slice(CUTS[n], CUTS[n + 1])
        groups.append(Gather(
            place, a_ref.at[:, cols],
            lambda top, size, cols=cols: m.at[pl.ds(top, size), cols],
            held, send.at[n], recv.at[n], needs[n], True,
        ))
    mine = pltpu.make_async_copy(a_ref, m.at[own_rows, :], extra)

    barrier = pltpu.get_barrier_semaphore()
    peers = place.f_dev + place.s_dev + place.far_dev + [place.twin]
    for dev in peers:
        pl.semaphore_signal(barrier, inc=1, device_id=dev, device_id_type=MESH)
    mine.start()
    pl.semaphore_wait(barrier, len(peers))

    first, mid, late, last = groups
    first.begin()
    m[order:, :] = b_ref[...]
    keep[...] = jnp.zeros_like(keep)
    work[DB:, :] = jnp.zeros((8, 2 * DB), f32)
    first.sides()
    first.far()
    mid.begin()
    first.second(0)
    first.second(1)
    first.second(2)
    first.third(0)
    first.third(1)
    first.second(3)
    first.third(2)
    first.third(3)
    late.begin()
    last.begin()
    first.close()
    mine.wait()

    plan = {
        (0, 0): [mid.sides, mid.far],
        (0, 1): [lambda: mid.second(0), lambda: mid.second(1), lambda: mid.second(2), late.sides],
        (0, 2): [lambda: mid.third(0), lambda: mid.third(1), lambda: mid.second(3), lambda: late.second(0), late.far],
        (0, 3): [lambda: mid.third(2), lambda: mid.third(3), lambda: late.second(1), lambda: late.third(0)],
        (0, 4): [mid.close, last.sides],
        (0, 5): [lambda: late.second(2), lambda: late.third(1)],
        (1, 0): [lambda: late.second(3), lambda: late.third(2), lambda: last.second(0)],
        (1, 1): [lambda: late.third(3), last.far],
        (1, 2): [lambda: last.second(1), lambda: last.third(0)],
        (1, 4): [late.close],
        (1, 5): [lambda: last.second(2), lambda: last.third(1)],
        (2, 1): [lambda: last.second(3), lambda: last.third(2)],
        (2, 3): [lambda: last.third(3)],
        (2, 4): [last.close],
    }

    def update(q, j):
        j2 = j + PB
        qs = slice(q * PB, q * PB + PB)
        right = jnp.concatenate([p_hi[j:j2, qs], p_lo[j:j2, qs], p_hi[j:j2, qs]], axis=1)
        left = jnp.concatenate([p_hi[j:, qs], p_hi[j:, qs], p_lo[j:, qs]], axis=1)
        m[j:, j:j2] = m[j:, j:j2] - nt(left, right)

    for p in range(order // PB):
        count = [0]

        def pause():
            for action in plan.get((p, count[0]), ()):
                action()
            count[0] += 1

        c0 = p * PB
        c1 = c0 + DB
        c2 = c0 + PB
        work[:DB, :DB] = m[c0:c1, c0:c1]
        work[:DB, DB:] = eye
        factor_corner(work, keep, pause)
        l11 = jnp.where(low_mask, work[:DB, :DB].T, 0.0)
        i11 = work[:DB, DB:]
        l21 = nt3(m[c1:c2, c0:c1], i11)
        work[:DB, :DB] = m[c1:c2, c1:c2] - nt3(l21, l21)
        work[:DB, DB:] = eye
        m[c0:c1, c0:c1] = l11
        m[c0:c1, c1:c2] = zero
        m[c1:c2, c0:c1] = l21
        inv[c0:c1, :DB] = i11
        inv[c0:c1, DB:] = zero
        factor_corner(work, keep, pause)
        l22 = jnp.where(low_mask, work[:DB, :DB].T, 0.0)
        i22 = work[:DB, DB:]
        i21 = -nn3(i22, nn3(m[c1:c2, c0:c1], inv[c0:c1, :DB]))
        m[c1:c2, c1:c2] = l22
        inv[c1:c2, :DB] = i21
        inv[c1:c2, DB:] = i22
        panel = nt3(m[c2:, c0:c2], inv[c0:c2, :])
        m[c2:, c0:c2] = panel
        hi, lo = two_terms(panel)
        p_hi[c2:, c0:c2] = hi
        p_lo[c2:, c0:c2] = lo
        pause()
        for j in range(c2, order, PB):
            opens = max(CUTS[n] for n in range(4) if CUTS[n] <= j)
            due = {256: 0, 512: 1, 1024: 2}[opens]
            if p == due:
                for q in range(p):
                    update(q, j)
            if p >= due:
                update(p, j)
        pause()
    x_ref[...] = m[order:, :]
    own = m[own_rows, :]
    row_id = lax.broadcasted_iota(jnp.int32, own.shape, 0) + spot * held
    col_id = lax.broadcasted_iota(jnp.int32, own.shape, 1)
    l_ref[...] = jnp.where(col_id <= row_id, own, 0.0)
    for p in reversed(range(order // PB)):
        c0 = p * PB
        c2 = c0 + PB
        rhs = m[order:, c0:c2]
        if c2 < order:
            rhs = rhs - nn3(m[order:, c2:], m[c2:order, c0:c2])
        g = nn3(rhs, inv[c0:c2, :])
        m[order:, c0:c2] = g
        g_ref[:, c0:c2] = g.astype(bf16)


def factor(a, b):
    held, order = a.shape
    rows = b.shape[0]
    vm = pl.BlockSpec(memory_space=pltpu.VMEM)
    return pl.pallas_call(
        functools.partial(factor_kernel, order, rows),
        out_shape=(
            jax.ShapeDtypeStruct((held, order), f32),
            jax.ShapeDtypeStruct((rows, order), f32),
            jax.ShapeDtypeStruct((rows, order), bf16),
        ),
        in_specs=[vm, vm],
        out_specs=(vm, vm, vm),
        scratch_shapes=[
            pltpu.VMEM((order + rows, order), f32),
            pltpu.VMEM((DB + 8, 2 * DB), f32),
            pltpu.VMEM((DB, 2 * DB), f32),
            pltpu.VMEM((order, PB), f32),
            pltpu.VMEM((order + rows, order), bf16),
            pltpu.VMEM((order + rows, order), bf16),
            pltpu.SemaphoreType.DMA((4, 36)),
            pltpu.SemaphoreType.DMA((4, 36)),
            pltpu.SemaphoreType.DMA,
        ],
        compiler_params=pltpu.CompilerParams(
            vmem_limit_bytes=60 * 2**20, collective_id=0, has_side_effects=True
        ),
        cost_estimate=pl.CostEstimate(flops=100 * 10**9, bytes_accessed=2 * 10**7, transcendentals=0),
        name="factor",
    )(a, b)


GROUP = 2


def tables(rows_ref, cols_ref, part, height, width):
    rows = rows_ref.shape[1]
    cols = cols_ref.shape[2]
    row_table = (lax.broadcasted_iota(jnp.int32, (height, rows), 0) == rows_ref[...]).astype(bf16)
    col_table = (lax.broadcasted_iota(jnp.int32, (width, cols), 0) == cols_ref[part]).astype(bf16)
    return row_table, col_table


def send_kernel(pick, g_ref, b_ref, c_ref, out_ref):
    out_ref[...] = (c_ref[...] - nt(g_ref[...], b_ref[...])).astype(bf16)


def keep_kernel(pick, g_ref, b_ref, c_ref, rows_ref, cols_ref, base_ref, out_ref):
    height, width = base_ref.shape
    width //= GROUP
    wide = cols_ref.shape[2]
    schur = c_ref[...] - nt(g_ref[...], b_ref[...])
    for part in range(GROUP):
        row_table, col_table = tables(rows_ref, cols_ref, part, height, width)
        high, low = two_terms(schur[:, part * wide:part * wide + wide])
        high = nt(high, col_table).astype(bf16)
        low = nt(low, col_table).astype(bf16)
        here = slice(part * width, part * width + width)
        out_ref[:, here] = base_ref[:, here] + (nn(row_table, high) + nn(row_table, low))


def join_kernel(s_ref, rows_ref, cols_ref, base_ref, out_ref):
    height, width = base_ref.shape
    width //= GROUP
    wide = cols_ref.shape[2]
    for part in range(GROUP):
        row_table, col_table = tables(rows_ref, cols_ref, part, height, width)
        here = slice(part * width, part * width + width)
        spread = nt(s_ref[:, part * wide:part * wide + wide], col_table).astype(bf16)
        out_ref[:, here] = base_ref[:, here] + nn(row_table, spread)


def cost(flops):
    return pl.CostEstimate(flops=flops, bytes_accessed=10**7, transcendentals=0)


def send_part(pick, g, b_all, c, wide, steps):
    rows, order = g.shape
    return pl.pallas_call(
        send_kernel,
        out_shape=jax.ShapeDtypeStruct((rows, wide * steps), bf16),
        grid_spec=pltpu.PrefetchScalarGridSpec(
            num_scalar_prefetch=1,
            grid=(steps,),
            in_specs=[
                pl.BlockSpec((rows, order), lambda t, pick: (0, 0)),
                pl.BlockSpec((wide, order), lambda t, pick: (pick[0] + t, 0)),
                pl.BlockSpec((rows, wide), lambda t, pick: (0, pick[0] + t)),
            ],
            out_specs=pl.BlockSpec((rows, wide), lambda t, pick: (0, t)),
        ),
        cost_estimate=cost(10**9),
        name="send_part",
    )(pick, g, b_all, c)


def keep_part(pick, g, b_all, c, row_link, col_link, base):
    steps, _, wide = col_link.shape
    rows, order = g.shape
    height, full = base.shape
    window = full // steps * GROUP
    steps //= GROUP
    block = wide * GROUP
    return pl.pallas_call(
        keep_kernel,
        out_shape=jax.ShapeDtypeStruct(base.shape, f32),
        grid_spec=pltpu.PrefetchScalarGridSpec(
            num_scalar_prefetch=1,
            grid=(steps,),
            in_specs=[
                pl.BlockSpec((rows, order), lambda t, pick: (0, 0)),
                pl.BlockSpec((block, order), lambda t, pick: (pick[0] + t, 0)),
                pl.BlockSpec((rows, block), lambda t, pick: (0, pick[0] + t)),
                pl.BlockSpec((1, rows), lambda t, pick: (0, 0)),
                pl.BlockSpec((GROUP, 1, wide), lambda t, pick: (t, 0, 0)),
                pl.BlockSpec((height, window), lambda t, pick: (0, t)),
            ],
            out_specs=pl.BlockSpec((height, window), lambda t, pick: (0, t)),
        ),
        cost_estimate=cost(5 * 10**9),
        name="keep_part",
    )(pick, g, b_all, c, row_link, col_link, base)


def join_part(part, parts, got, row_link, col_link, base):
    steps, _, wide = col_link.shape
    rows = got.shape[0]
    height, full = base.shape
    window = full // steps * GROUP
    steps //= GROUP
    block = wide * GROUP
    count = steps // parts
    first = part * count
    return pl.pallas_call(
        join_kernel,
        out_shape=jax.ShapeDtypeStruct(base.shape, f32),
        grid=(count,),
        in_specs=[
            pl.BlockSpec((rows, block), lambda t: (0, t)),
            pl.BlockSpec((1, rows), lambda t: (0, 0)),
            pl.BlockSpec((GROUP, 1, wide), lambda t: (t + first, 0, 0)),
            pl.BlockSpec((height, window), lambda t: (0, t + first)),
        ],
        out_specs=pl.BlockSpec((height, window), lambda t: (0, t + first)),
        input_output_aliases={3: 0},
        cost_estimate=cost(10**9),
        name="join_part",
    )(got, row_link, col_link, base)


AXES = ("leaf", "prow", "pcol")


def local(front_pivot, front_lower, front_rest, parent_front, relation):
    position = lax.axis_index(("prow", "pcol"))
    leaf = lax.axis_index("leaf")
    spots = lax.axis_size("prow") * lax.axis_size("pcol")
    leaves = lax.axis_size("leaf")
    side = leaf % 2
    partner = leaf + 1 - 2 * side
    pivot_rows = front_pivot[0]
    lower_rows = front_lower[0]
    rest_rows = front_rest[0]
    base = parent_front[0]
    rows_here, child_order = rest_rows.shape
    half = child_order // 2
    height, parent_half = base.shape
    steps = 8
    wide = half // steps
    window = parent_half // steps


    mirror = [(one * spots + spot, (one ^ 1) * spots + spot) for one in range(leaves) for spot in range(spots)]
    b_all = lax.all_gather(lower_rows.astype(bf16), ("prow", "pcol"), axis=0, tiled=True)
    pivot_out, lower_out, g = factor(pivot_rows, lower_rows)

    def links(child):
        link = lax.dynamic_index_in_dim(relation, child, 0, keepdims=False)
        row_link = lax.dynamic_slice_in_dim(link, position * rows_here, rows_here, 0) - position * height
        col_link = lax.dynamic_slice_in_dim(link, side * half, half, 0) - side * parent_half
        col_link = col_link.reshape(steps, 1, wide) - jnp.arange(steps, dtype=jnp.int32)[:, None, None] * window
        return row_link[None], col_link

    row_own, col_own = links(leaf)
    row_sib, col_sib = links(partner)
    received = []
    parts = 2
    for part in range(parts):
        pick = jnp.full((1,), ((1 - side) * steps + part * (steps // parts)) // GROUP, jnp.int32)
        sent = send_part(pick, g, b_all, rest_rows, wide * GROUP, steps // parts // GROUP)
        received.append(lax.ppermute(sent, AXES, mirror))
    merged = keep_part(jnp.full((1,), side * steps // GROUP, jnp.int32), g, b_all, rest_rows, row_own, col_own, base)
    for part in range(parts):
        merged = join_part(part, parts, received[part], row_sib, col_sib, merged)
    return (pivot_out[None], lower_out[None], merged[None])


def solution(mesh):
    spec = P("leaf", ("prow", "pcol"), None)
    return jax.shard_map(
        local,
        mesh=mesh,
        in_specs=(spec, spec, spec, spec, P()),
        out_specs=(spec, spec, spec),
        check_vma=False,
    )
```

```python
import functools

import jax
import jax.numpy as jnp
from jax import lax
from jax.experimental import pallas as pl
from jax.experimental.pallas import tpu as pltpu
from jax.sharding import PartitionSpec as P

DB = 128
PB = 256
f32 = jnp.float32
bf16 = jnp.bfloat16


def two_terms(value):
    high = value.astype(bf16)
    low = (value - high.astype(f32)).astype(bf16)
    return high, low


def nt(a, b):
    return lax.dot_general(a, b, (((1,), (1,)), ((), ())), preferred_element_type=f32)


def nn(a, b):
    return lax.dot_general(a, b, (((1,), (0,)), ((), ())), preferred_element_type=f32)


def left3(value):
    high, low = two_terms(value)
    return jnp.concatenate([high, high, low], axis=1)


def right3(value, axis=1):
    high, low = two_terms(value)
    return jnp.concatenate([high, low, high], axis=axis)


def nt3(a, b):
    return nt(left3(a), right3(b))


def nn3(a, b):
    return nn(left3(a), right3(b, 0))


def factor_corner(work, keep, pause, segments=2):
    count = DB // 8
    sub = lax.broadcasted_iota(jnp.int32, (8, DB), 0)

    def wide(row):
        return jnp.broadcast_to(row, (8, DB))

    def step(first, block, carry):
        start = pl.multiple_of(block * 8, 8)
        after = pl.multiple_of(start + 8, 8)
        before = pl.multiple_of(jnp.maximum(start - 8, 0), 8)
        started = jnp.where(block > 0, 1.0, 0.0).astype(f32)
        halves = (slice(0, DB), slice(DB, 2 * DB))
        rows = [work[pl.ds(start, 8), h] for h in halves]
        tile = [work[pl.ds(after, 8), h] for h in halves]
        past = [keep[pl.ds(before, 8), h] for h in halves]
        lane = jnp.zeros((8, DB), jnp.int32) + start
        lane_before = jnp.zeros((8, DB), jnp.int32) + before

        low = (first + 1) * 8
        if low < DB:
            left = work[low:DB, :DB]
            place = lax.broadcasted_iota(jnp.int32, left.shape, 1)
            depth = lax.broadcasted_iota(jnp.int32, left.shape, 0) + low
            chosen = (place >= start - 8) & (place < start) & (depth >= start + 16)
            left = jnp.where(chosen, left, 0.0)
            change = nn3(left, keep[...])

        for k in range(8):
            coef = jnp.take_along_axis(tile[0], lane_before + k, axis=1) * started
            if k == 0:
                drop = [coef * wide(past[s][k:k + 1]) for s in range(2)]
            else:
                drop = [drop[s] + coef * wide(past[s][k:k + 1]) for s in range(2)]
        tile = [tile[s] - drop[s] for s in range(2)]

        a = {}
        side_col = []
        for k in range(8):
            piece = jnp.take_along_axis(rows[0], lane + k, axis=1)
            for s in range(k, 8):
                a[s, k] = wide(piece[s:s + 1])
            side_col.append(jnp.take_along_axis(tile[0], lane + k, axis=1))
        r = []
        up = []
        for i in range(8):
            inv = lax.rsqrt(a[i, i])
            r.append(inv)
            for k in range(i + 1, 8):
                a[k, i] = a[k, i] * inv
            for k in range(i + 1, 8):
                for j in range(i + 1, k + 1):
                    a[k, j] = a[k, j] - a[k, i] * a[j, i]
            side_col[i] = side_col[i] * inv
            for k in range(i + 1, 8):
                side_col[k] = side_col[k] - a[k, i] * side_col[i]
            if i == 0:
                run = [[wide(rows[s][k:k + 1]) for k in range(8)] for s in range(2)]
            pair = []
            for s in range(2):
                value = run[s][i] * inv
                pair.append(value)
                for k in range(i + 1, 8):
                    run[s][k] = run[s][k] - a[k, i] * value
                tile[s] = tile[s] - side_col[i] * value
            up.append(pair)
        if low < DB:
            work[low:DB, :] = work[low:DB, :] - change
        for s in range(2):
            work[pl.ds(after, 8), halves[s]] = tile[s]
            value = up[0][s]
            for i in range(1, 8):
                value = jnp.where(sub == i, up[i][s], value)
            work[pl.ds(start, 8), halves[s]] = value
        back = [None] * 8
        for i in reversed(range(8)):
            pair = []
            for s in range(2):
                value = up[i][s]
                for k in reversed(range(i + 1, 8)):
                    value = value - a[k, i] * back[k][s]
                pair.append(value * r[i])
            back[i] = pair
        for s in range(2):
            value = back[0][s]
            for i in range(1, 8):
                value = jnp.where(sub == i, back[i][s], value)
            keep[pl.ds(start, 8), halves[s]] = value
        return carry

    size = count // segments
    for seg in range(segments):
        lax.fori_loop(seg * size, (seg + 1) * size, lambda b, c, f=seg * size: step(f, b, c), 0)
        pause()


MESH = pl.DeviceIdType.MESH
RING = 4


class Place:
    def __init__(self):
        self.leaf = lax.axis_index("leaf")
        self.z = lax.axis_index("prow")
        pcol = lax.axis_index("pcol")
        self.x = pcol // 2
        self.core = pcol % 2
        self.flip = self.core == 1
        self.f = jnp.where(self.flip, self.z, self.x)
        self.s = jnp.where(self.flip, self.x, self.z)
        self.f_dev = [self.device(self.near(self.f, 1), self.s), self.device(self.near(self.f, -1), self.s)]
        self.s_dev = [self.device(self.f, self.near(self.s, 1)), self.device(self.f, self.near(self.s, -1))]
        self.twin = (self.leaf, self.z, self.x * 2 + 1 - self.core)
        self.far_dev = [self.device(self.near(self.f, 2), self.s), self.device(self.f, self.near(self.s, 2))]

    def near(self, v, d):
        return (v + d + RING) % RING

    def chip(self, fi, si):
        return jnp.where(self.flip, fi, si), jnp.where(self.flip, si, fi)

    def device(self, fi, si):
        zi, xi = self.chip(fi, si)
        return (self.leaf, zi, xi * 2 + self.core)


class Gather:
    OFFSETS = (0, -1, 1, 2)

    def __init__(self, place, source, view, rows, send, recv, needed=None, direct=False):
        self.place = place
        self.source = source
        self.view = view
        self.rows = rows
        self.send = send
        self.recv = recv
        self.needed = needed
        self.direct = direct
        self.started = []

    def window(self, fi, si, piece=None, twin=False):
        p = self.place
        zi, xi = p.chip(fi, si)
        slot = zi * 2 * RING + xi * 2 + ((1 - p.core) if twin else p.core)
        top = slot * self.rows
        part = self.rows // 2
        if piece is None:
            return self.view(pl.multiple_of(top, 8), self.rows)
        return self.view(pl.multiple_of(top + piece * part, 8), part)

    def under(self, fi, si, action):
        if self.needed is None:
            action()
        else:
            pl.when(self.needed(self.place.chip(fi, si)[0]))(action)

    def push(self, fi, si, src, dst, sem, dev):
        copy = pltpu.make_async_remote_copy(
            src_ref=src, dst_ref=dst, send_sem=self.send.at[len(self.started)],
            recv_sem=self.recv.at[sem], device_id=dev, device_id_type=MESH,
        )
        self.started.append((fi, si, copy))
        self.under(fi, si, copy.start)

    def arrived(self, fi, si, dst, sem):
        copy = pltpu.make_async_remote_copy(
            src_ref=dst, dst_ref=dst, send_sem=self.send.at[0],
            recv_sem=self.recv.at[sem], device_id=self.place.twin, device_id_type=MESH,
        )
        self.under(fi, si, copy.wait_recv)

    def f_sem(self, d):
        return d

    def s_sem(self, k, d):
        return 4 + 4 * k + d

    def c_sem(self, a, k):
        return 20 + 4 * a + k

    def pass_on(self, k, src, fi):
        p = self.place
        dst = self.window(fi, p.s)
        for d in range(2):
            self.push(fi, p.s, src, dst, self.s_sem(k, d), p.s_dev[d])
        if self.direct:
            self.push(fi, p.s, src, dst, self.s_sem(k, 2), p.far_dev[1])
        self.push(fi, p.s, src, dst, self.c_sem(0, k), p.twin)

    def begin(self):
        p = self.place
        for d in range(2):
            self.push(p.f, p.s, self.source, self.window(p.f, p.s), self.f_sem(d), p.f_dev[d])
        if self.direct:
            self.push(p.f, p.s, self.source, self.window(p.f, p.s), self.f_sem(2), p.far_dev[0])
        self.pass_on(0, self.source, p.f)

    def sides(self):
        p = self.place
        for d, off in ((0, -1), (1, 1)):
            fi = p.near(p.f, off)
            self.arrived(fi, p.s, self.window(fi, p.s), self.f_sem(d))
            if not self.direct:
                half = self.window(fi, p.s, d)
                self.push(fi, p.s, half, half, self.f_sem(2 + d), p.f_dev[d])
            self.pass_on(1 + d, self.window(fi, p.s), fi)

    def far(self):
        p = self.place
        fi = p.near(p.f, 2)
        if self.direct:
            self.arrived(fi, p.s, self.window(fi, p.s), self.f_sem(2))
        else:
            for d in range(2):
                self.arrived(fi, p.s, self.window(fi, p.s, d), self.f_sem(2 + d))
        self.pass_on(3, self.window(fi, p.s), fi)

    def second(self, k):
        p = self.place
        fi = p.near(p.f, self.OFFSETS[k])
        for d, off in ((0, -1), (1, 1)):
            si = p.near(p.s, off)
            self.arrived(fi, si, self.window(fi, si), self.s_sem(k, d))
            if not self.direct:
                half = self.window(fi, si, d)
                self.push(fi, si, half, half, self.s_sem(k, 2 + d), p.s_dev[d])
            whole = self.window(fi, si)
            self.push(fi, si, whole, whole, self.c_sem(1 + d, k), p.twin)

    def third(self, k):
        p = self.place
        fi = p.near(p.f, self.OFFSETS[k])
        si = p.near(p.s, 2)
        if self.direct:
            self.arrived(fi, si, self.window(fi, si), self.s_sem(k, 2))
        else:
            for d in range(2):
                self.arrived(fi, si, self.window(fi, si, d), self.s_sem(k, 2 + d))
        whole = self.window(fi, si)
        self.push(fi, si, whole, whole, self.c_sem(3, k), p.twin)

    def close(self):
        p = self.place
        for a in range(4):
            for b in range(4):
                fi = p.near(p.f, self.OFFSETS[a])
                si = p.near(p.s, self.OFFSETS[b])
                self.arrived(fi, si, self.window(fi, si, twin=True), self.c_sem(a, b))
        for fi, si, copy in self.started:
            self.under(fi, si, copy.wait_send)


CUTS = (0, 256, 512, 1024, 1536)


def factor_kernel(
    order, rows, a_ref, b_ref, l_ref, x_ref, g_ref,
    m, work, keep, inv, p_hi, p_lo, send, recv, extra,
):
    place = Place()
    held = l_ref.shape[0]
    eye = (lax.broadcasted_iota(jnp.int32, (DB, DB), 0) == lax.broadcasted_iota(jnp.int32, (DB, DB), 1)).astype(f32)
    low_mask = lax.broadcasted_iota(jnp.int32, (DB, DB), 0) >= lax.broadcasted_iota(jnp.int32, (DB, DB), 1)
    zero = jnp.zeros((DB, DB), f32)

    spot = place.z * 2 * RING + place.x * 2 + place.core
    own_rows = pl.ds(pl.multiple_of(spot * held, 8), held)

    groups = []
    needs = (None, None, lambda zi: zi >= 1, lambda zi: zi >= 2)
    for n in range(4):
        cols = slice(CUTS[n], CUTS[n + 1])
        groups.append(Gather(
            place, a_ref.at[:, cols],
            lambda top, size, cols=cols: m.at[pl.ds(top, size), cols],
            held, send.at[n], recv.at[n], needs[n], True,
        ))
    mine = pltpu.make_async_copy(a_ref, m.at[own_rows, :], extra)

    barrier = pltpu.get_barrier_semaphore()
    peers = place.f_dev + place.s_dev + place.far_dev + [place.twin]
    for dev in peers:
        pl.semaphore_signal(barrier, inc=1, device_id=dev, device_id_type=MESH)
    mine.start()
    pl.semaphore_wait(barrier, len(peers))

    first, mid, late, last = groups
    first.begin()
    m[order:, :] = b_ref[...]
    keep[...] = jnp.zeros_like(keep)
    work[DB:, :] = jnp.zeros((8, 2 * DB), f32)
    first.sides()
    first.far()
    mid.begin()
    first.second(0)
    first.second(1)
    first.second(2)
    first.third(0)
    first.third(1)
    first.second(3)
    first.third(2)
    first.third(3)
    late.begin()
    last.begin()
    first.close()
    mine.wait()

    plan = {
        (0, 0): [mid.sides, mid.far],
        (0, 1): [lambda: mid.second(0), lambda: mid.second(1), lambda: mid.second(2), late.sides],
        (0, 2): [lambda: mid.third(0), lambda: mid.third(1), lambda: mid.second(3), lambda: late.second(0), late.far],
        (0, 3): [lambda: mid.third(2), lambda: mid.third(3), lambda: late.second(1), lambda: late.third(0)],
        (0, 4): [mid.close, last.sides],
        (0, 5): [lambda: late.second(2), lambda: late.third(1)],
        (1, 0): [lambda: late.second(3), lambda: late.third(2), lambda: last.second(0)],
        (1, 1): [lambda: late.third(3), last.far],
        (1, 2): [lambda: last.second(1), lambda: last.third(0)],
        (1, 4): [late.close],
        (1, 5): [lambda: last.second(2), lambda: last.third(1)],
        (2, 1): [lambda: last.second(3), lambda: last.third(2)],
        (2, 3): [lambda: last.third(3)],
        (2, 4): [last.close],
    }

    def update(q, j):
        j2 = j + PB
        qs = slice(q * PB, q * PB + PB)
        right = jnp.concatenate([p_hi[j:j2, qs], p_lo[j:j2, qs], p_hi[j:j2, qs]], axis=1)
        left = jnp.concatenate([p_hi[j:, qs], p_hi[j:, qs], p_lo[j:, qs]], axis=1)
        m[j:, j:j2] = m[j:, j:j2] - nt(left, right)

    for p in range(order // PB):
        count = [0]

        def pause():
            for action in plan.get((p, count[0]), ()):
                action()
            count[0] += 1

        c0 = p * PB
        c1 = c0 + DB
        c2 = c0 + PB
        work[:DB, :DB] = m[c0:c1, c0:c1]
        work[:DB, DB:] = eye
        factor_corner(work, keep, pause)
        l11 = jnp.where(low_mask, work[:DB, :DB].T, 0.0)
        i11 = work[:DB, DB:]
        l21 = nt3(m[c1:c2, c0:c1], i11)
        work[:DB, :DB] = m[c1:c2, c1:c2] - nt3(l21, l21)
        work[:DB, DB:] = eye
        m[c0:c1, c0:c1] = l11
        m[c0:c1, c1:c2] = zero
        m[c1:c2, c0:c1] = l21
        inv[c0:c1, :DB] = i11
        inv[c0:c1, DB:] = zero
        factor_corner(work, keep, pause)
        l22 = jnp.where(low_mask, work[:DB, :DB].T, 0.0)
        i22 = work[:DB, DB:]
        i21 = -nn3(i22, nn3(m[c1:c2, c0:c1], inv[c0:c1, :DB]))
        m[c1:c2, c1:c2] = l22
        inv[c1:c2, :DB] = i21
        inv[c1:c2, DB:] = i22
        panel = nt3(m[c2:, c0:c2], inv[c0:c2, :])
        m[c2:, c0:c2] = panel
        hi, lo = two_terms(panel)
        p_hi[c2:, c0:c2] = hi
        p_lo[c2:, c0:c2] = lo
        pause()
        for j in range(c2, order, PB):
            opens = max(CUTS[n] for n in range(4) if CUTS[n] <= j)
            due = {256: 0, 512: 1, 1024: 2}[opens]
            if p == due:
                for q in range(p):
                    update(q, j)
            if p >= due:
                update(p, j)
        pause()
    x_ref[...] = m[order:, :]
    own = m[own_rows, :]
    row_id = lax.broadcasted_iota(jnp.int32, own.shape, 0) + spot * held
    col_id = lax.broadcasted_iota(jnp.int32, own.shape, 1)
    l_ref[...] = jnp.where(col_id <= row_id, own, 0.0)
    for p in reversed(range(order // PB)):
        c0 = p * PB
        c2 = c0 + PB
        rhs = m[order:, c0:c2]
        if c2 < order:
            rhs = rhs - nn3(m[order:, c2:], m[c2:order, c0:c2])
        g = nn3(rhs, inv[c0:c2, :])
        m[order:, c0:c2] = g
        g_ref[:, c0:c2] = g.astype(bf16)


def factor(a, b):
    held, order = a.shape
    rows = b.shape[0]
    vm = pl.BlockSpec(memory_space=pltpu.VMEM)
    return pl.pallas_call(
        functools.partial(factor_kernel, order, rows),
        out_shape=(
            jax.ShapeDtypeStruct((held, order), f32),
            jax.ShapeDtypeStruct((rows, order), f32),
            jax.ShapeDtypeStruct((rows, order), bf16),
        ),
        in_specs=[vm, vm],
        out_specs=(vm, vm, vm),
        scratch_shapes=[
            pltpu.VMEM((order + rows, order), f32),
            pltpu.VMEM((DB + 8, 2 * DB), f32),
            pltpu.VMEM((DB, 2 * DB), f32),
            pltpu.VMEM((order, PB), f32),
            pltpu.VMEM((order + rows, order), bf16),
            pltpu.VMEM((order + rows, order), bf16),
            pltpu.SemaphoreType.DMA((4, 36)),
            pltpu.SemaphoreType.DMA((4, 36)),
            pltpu.SemaphoreType.DMA,
        ],
        compiler_params=pltpu.CompilerParams(
            vmem_limit_bytes=60 * 2**20, collective_id=0, has_side_effects=True
        ),
        cost_estimate=pl.CostEstimate(flops=100 * 10**9, bytes_accessed=2 * 10**7, transcendentals=0),
        name="factor",
    )(a, b)


GROUP = 2


def tables(rows_ref, cols_ref, part, height, width):
    rows = rows_ref.shape[1]
    cols = cols_ref.shape[2]
    row_table = (lax.broadcasted_iota(jnp.int32, (height, rows), 0) == rows_ref[...]).astype(bf16)
    col_table = (lax.broadcasted_iota(jnp.int32, (width, cols), 0) == cols_ref[part]).astype(bf16)
    return row_table, col_table


def send_kernel(pick, g_ref, b_ref, c_ref, out_ref):
    out_ref[...] = (c_ref[...] - nt(g_ref[...], b_ref[...])).astype(bf16)


def keep_kernel(pick, g_ref, b_ref, c_ref, rows_ref, cols_ref, base_ref, out_ref):
    height, width = base_ref.shape
    width //= GROUP
    wide = cols_ref.shape[2]
    schur = c_ref[...] - nt(g_ref[...], b_ref[...])
    for part in range(GROUP):
        row_table, col_table = tables(rows_ref, cols_ref, part, height, width)
        high, low = two_terms(schur[:, part * wide:part * wide + wide])
        high = nt(high, col_table).astype(bf16)
        low = nt(low, col_table).astype(bf16)
        here = slice(part * width, part * width + width)
        out_ref[:, here] = base_ref[:, here] + (nn(row_table, high) + nn(row_table, low))


def join_kernel(s_ref, rows_ref, cols_ref, base_ref, out_ref):
    height, width = base_ref.shape
    width //= GROUP
    wide = cols_ref.shape[2]
    for part in range(GROUP):
        row_table, col_table = tables(rows_ref, cols_ref, part, height, width)
        here = slice(part * width, part * width + width)
        spread = nt(s_ref[:, part * wide:part * wide + wide], col_table).astype(bf16)
        out_ref[:, here] = base_ref[:, here] + nn(row_table, spread)


def cost(flops):
    return pl.CostEstimate(flops=flops, bytes_accessed=10**7, transcendentals=0)


def send_part(pick, g, b_all, c, wide, steps):
    rows, order = g.shape
    return pl.pallas_call(
        send_kernel,
        out_shape=jax.ShapeDtypeStruct((rows, wide * steps), bf16),
        grid_spec=pltpu.PrefetchScalarGridSpec(
            num_scalar_prefetch=1,
            grid=(steps,),
            in_specs=[
                pl.BlockSpec((rows, order), lambda t, pick: (0, 0)),
                pl.BlockSpec((wide, order), lambda t, pick: (pick[0] + t, 0)),
                pl.BlockSpec((rows, wide), lambda t, pick: (0, pick[0] + t)),
            ],
            out_specs=pl.BlockSpec((rows, wide), lambda t, pick: (0, t)),
        ),
        cost_estimate=cost(10**9),
        name="send_part",
    )(pick, g, b_all, c)


def keep_part(pick, g, b_all, c, row_link, col_link, base):
    steps, _, wide = col_link.shape
    rows, order = g.shape
    height, full = base.shape
    window = full // steps * GROUP
    steps //= GROUP
    block = wide * GROUP
    return pl.pallas_call(
        keep_kernel,
        out_shape=jax.ShapeDtypeStruct(base.shape, f32),
        grid_spec=pltpu.PrefetchScalarGridSpec(
            num_scalar_prefetch=1,
            grid=(steps,),
            in_specs=[
                pl.BlockSpec((rows, order), lambda t, pick: (0, 0)),
                pl.BlockSpec((block, order), lambda t, pick: (pick[0] + t, 0)),
                pl.BlockSpec((rows, block), lambda t, pick: (0, pick[0] + t)),
                pl.BlockSpec((1, rows), lambda t, pick: (0, 0)),
                pl.BlockSpec((GROUP, 1, wide), lambda t, pick: (t, 0, 0)),
                pl.BlockSpec((height, window), lambda t, pick: (0, t)),
            ],
            out_specs=pl.BlockSpec((height, window), lambda t, pick: (0, t)),
        ),
        cost_estimate=cost(5 * 10**9),
        name="keep_part",
    )(pick, g, b_all, c, row_link, col_link, base)


def join_part(part, parts, got, row_link, col_link, base):
    steps, _, wide = col_link.shape
    rows = got.shape[0]
    height, full = base.shape
    window = full // steps * GROUP
    steps //= GROUP
    block = wide * GROUP
    count = steps // parts
    first = part * count
    return pl.pallas_call(
        join_kernel,
        out_shape=jax.ShapeDtypeStruct(base.shape, f32),
        grid=(count,),
        in_specs=[
            pl.BlockSpec((rows, block), lambda t: (0, t)),
            pl.BlockSpec((1, rows), lambda t: (0, 0)),
            pl.BlockSpec((GROUP, 1, wide), lambda t: (t + first, 0, 0)),
            pl.BlockSpec((height, window), lambda t: (0, t + first)),
        ],
        out_specs=pl.BlockSpec((height, window), lambda t: (0, t + first)),
        input_output_aliases={3: 0},
        cost_estimate=cost(10**9),
        name="join_part",
    )(got, row_link, col_link, base)


AXES = ("leaf", "prow", "pcol")


def local(front_pivot, front_lower, front_rest, parent_front, relation):
    position = lax.axis_index(("prow", "pcol"))
    leaf = lax.axis_index("leaf")
    spots = lax.axis_size("prow") * lax.axis_size("pcol")
    leaves = lax.axis_size("leaf")
    side = leaf % 2
    partner = leaf + 1 - 2 * side
    pivot_rows = front_pivot[0]
    lower_rows = front_lower[0]
    rest_rows = front_rest[0]
    base = parent_front[0]
    rows_here, child_order = rest_rows.shape
    half = child_order // 2
    height, parent_half = base.shape
    steps = 8
    wide = half // steps
    window = parent_half // steps


    mirror = [(one * spots + spot, (one ^ 1) * spots + spot) for one in range(leaves) for spot in range(spots)]
    b_all = lax.all_gather(lower_rows.astype(bf16), ("prow", "pcol"), axis=0, tiled=True)
    pivot_out, lower_out, g = factor(pivot_rows, lower_rows)

    def links(child):
        link = lax.dynamic_index_in_dim(relation, child, 0, keepdims=False)
        row_link = lax.dynamic_slice_in_dim(link, position * rows_here, rows_here, 0) - position * height
        col_link = lax.dynamic_slice_in_dim(link, side * half, half, 0) - side * parent_half
        col_link = col_link.reshape(steps, 1, wide) - jnp.arange(steps, dtype=jnp.int32)[:, None, None] * window
        return row_link[None], col_link

    row_own, col_own = links(leaf)
    row_sib, col_sib = links(partner)
    received = []
    parts = 2
    for part in range(parts):
        pick = jnp.full((1,), ((1 - side) * steps + part * (steps // parts)) // GROUP, jnp.int32)
        sent = send_part(pick, g, b_all, rest_rows, wide * GROUP, steps // parts // GROUP)
        received.append(lax.ppermute(sent, AXES, mirror))
    merged = keep_part(jnp.full((1,), side * steps // GROUP, jnp.int32), g, b_all, rest_rows, row_own, col_own, base)
    for part in reversed(range(parts)):
        merged = join_part(part, parts, received[part], row_sib, col_sib, merged)
    pivot_out, lower_out, sent = lax.optimization_barrier((pivot_out, lower_out, sent))
    pivot_out = jnp.where(position >= 0, pivot_out, 0.0)
    lower_out = jnp.where(position >= 0, lower_out, 0.0)
    return (pivot_out[None], lower_out[None], merged[None])


def solution(mesh):
    spec = P("leaf", ("prow", "pcol"), None)
    return jax.shard_map(
        local,
        mesh=mesh,
        in_specs=(spec, spec, spec, spec, P()),
        out_specs=(spec, spec, spec),
        check_vma=False,
    )
```
